32 devices in a mesh: seg: 4 (over y, x), slab: 8 (over z, core).
Axes of the slice: x: 2, y: 2, z: 4, core: 2. Of those that a mesh axis runs over, the one named last changes fastest.
Arguments:
- positions: bfloat16 [4, 32, 3, 642], P('seg', 'slab'), may hold values from -6 to 6
- density: bfloat16 [4, 32, 3, 642], P('seg', 'slab'), may hold values from -6 to 6
- upsample: bfloat16 [642, 2562], replicated, may hold values from -0.25 to 0.25
- quad_weights: float32 [2562], replicated, may hold values from 0.3 to 3
- coarse_weights: float32 [642], replicated, may hold values from 0.3 to 3
- pair_target: int32 [4, 16], P('seg', 'slab'), may hold values from 0 to 3
- pair_source: int32 [4, 16], P('seg', 'slab'), may hold values from 0 to 7
- junction_cell: int32 [4, 8, 4], P('seg', 'slab'), may hold values from 0 to 3
- junction_target: int32 [4, 8, 4], P('seg', 'slab'), may hold values from 0 to 3
- wall_points: bfloat16 [4, 8, 3, 128], P('seg', 'slab'), may hold values from -6 to 6
- wall_traction: bfloat16 [4, 8, 3, 128], P('seg', 'slab'), may hold values from -6 to 6
- wall_near: int32 [4, 32, 2], P('seg', 'slab'), may hold values from 0 to 7
Outputs:
- velocity: float32 [4, 32, 3, 642], P('seg', 'slab')
The draws below stay inside these ranges and needn't reach their ends.
All inputs are finite; a program needn't handle non-finite values.
Results may differ from the reference program's by a relative error of at most 0.0024.
Values may be sent and summed in bfloat16 or wider, within the bound.
A program may use at most 64 MiB of HBM per device.

```python
import math
import jax
import jax.numpy as jnp
from jax import lax

P_SIZE = 642
Q = 2562
WP = 128
CELL_DEV = 4
HALO = 2
NEAR = 2
PAIRS_DEV = 2
CELLS_SEG = 32
PATCHES_SEG = 8
N_SEG = 4
N_SLAB = 8


def set_ends(values, key, least, top_value):
    index_at = [jax.random.randint(jax.random.fold_in(key, axis), (), 0, length) for axis, length in enumerate(values.shape)]
    widest = values.shape.index(max(values.shape))
    beside = index_at[:widest] + [(index_at[widest] + 1) % values.shape[widest]] + index_at[widest + 1:]
    return values.at[tuple(index_at)].set(least).at[tuple(beside)].set(top_value)


def block_levels(own_key, dims, pieces, smallest, top_value):
    def one(axis_at, shards_of):
        draws = jax.random.uniform(jax.random.fold_in(jax.random.fold_in(own_key, 6), axis_at), (shards_of,), jnp.float32, smallest / len(pieces), top_value / len(pieces))
        return jnp.repeat(jnp.exp(draws), dims[axis_at] // shards_of).reshape((-1,) + (1,) * (len(dims) - axis_at - 1))

    level = one(*pieces[0])
    for cut in pieces[1:]:
        level = level * one(*cut)
    return level


def scatter_about(own_key, extent, scale, limit, split=(), kind=jnp.bfloat16):
    values = jax.random.normal(own_key, extent, jnp.float32) * scale
    if len(split) > 0:
        values = block_levels(own_key, extent, split, -0.22, 0.18) * values
    return jnp.clip(values, min=-limit, max=limit).astype(kind)


def setup_inputs(seed: int = 0) -> dict:
    key_list = jax.random.split(jax.random.key(seed), 13)
    return {
        "positions": scatter_about(key_list[0], (N_SEG, CELLS_SEG, 3, P_SIZE), 1.0, 6.0, ((0, 4), (1, 8))),
        "density": scatter_about(key_list[1], (N_SEG, CELLS_SEG, 3, P_SIZE), 1.0, 6.0, ((0, 4), (1, 8))),
        "upsample": scatter_about(key_list[2], (P_SIZE, Q), P_SIZE ** -0.5, 0.25),
        "quad_weights": jnp.clip(jnp.exp(jax.random.uniform(key_list[3], (Q,), jnp.float32, math.log(0.3), math.log(3.0))), 0.3, 3.0),
        "coarse_weights": jnp.clip(jnp.exp(jax.random.uniform(key_list[4], (P_SIZE,), jnp.float32, math.log(0.3), math.log(3.0))), 0.3, 3.0),
        "pair_target": set_ends(jax.random.randint(key_list[5], (N_SEG, N_SLAB * PAIRS_DEV), 0, CELL_DEV), jax.random.fold_in(key_list[5], 1), 0, CELL_DEV - 1).astype(jnp.int32),
        "pair_source": set_ends(jax.random.randint(key_list[6], (N_SEG, N_SLAB * PAIRS_DEV), 0, CELL_DEV + 2 * HALO), jax.random.fold_in(key_list[6], 1), 0, (CELL_DEV + 2 * HALO) - 1).astype(jnp.int32),
        "junction_cell": set_ends(jax.random.randint(key_list[7], (N_SEG, N_SLAB, N_SEG), 0, CELL_DEV), jax.random.fold_in(key_list[7], 1), 0, CELL_DEV - 1).astype(jnp.int32),
        "junction_target": set_ends(jax.random.randint(key_list[8], (N_SEG, N_SLAB, N_SEG), 0, CELL_DEV), jax.random.fold_in(key_list[8], 1), 0, CELL_DEV - 1).astype(jnp.int32),
        "wall_points": scatter_about(key_list[9], (N_SEG, PATCHES_SEG, 3, WP), 1.0, 6.0, ((0, 4), (1, 8))),
        "wall_traction": scatter_about(key_list[10], (N_SEG, PATCHES_SEG, 3, WP), 1.0, 6.0, ((0, 4), (1, 8))),
        "wall_near": set_ends(jax.random.randint(key_list[11], (N_SEG, CELLS_SEG, NEAR), 0, PATCHES_SEG), jax.random.fold_in(key_list[11], 1), 0, PATCHES_SEG - 1).astype(jnp.int32),
    }


EPSILON2 = 0.05
WALL_GAIN = 3.0

def kernel_rows(targets, sources, strength):
    offset = targets[:, :, None] - sources[:, None, :]
    distance2 = lax.optimization_barrier(jnp.sum(offset * offset, axis=0))
    inverse = lax.rsqrt(distance2 + EPSILON2)
    inverse3 = inverse * inverse * inverse
    along_offset = lax.optimization_barrier(jnp.sum(offset * strength[:, None, :], axis=0))
    summand = (strength[:, None, :] * (distance2 + 2.0 * EPSILON2) + along_offset[None] * offset) * inverse3[None]
    return lax.optimization_barrier(jnp.sum(summand, axis=2)) / (8.0 * math.pi)

def grouped(func, operands, group):
    total = operands[0].shape[0]
    shaped = jax.tree.map(lambda leaf_array: leaf_array.reshape((total // group, group) + leaf_array.shape[1:]), operands)
    result = lax.map(lambda batch: jax.vmap(func)(*batch), shaped)
    return result.reshape((total,) + result.shape[2:])

def reference(positions, density, upsample, quad_weights, coarse_weights, pair_target, pair_source, junction_cell, junction_target, wall_points, wall_traction, wall_near):
    cell_seg = N_SLAB * CELL_DEV
    upsample_full = upsample.astype(jnp.float32)
    fine_points = jnp.einsum('gckp,pq->gckq', positions.astype(jnp.float32), upsample_full, precision=lax.Precision.HIGHEST).astype(jnp.bfloat16)
    fine_density = jnp.einsum('gckp,pq->gckq', density.astype(jnp.float32), upsample_full, precision=lax.Precision.HIGHEST).astype(jnp.bfloat16)
    velocity = jnp.zeros(positions.shape, jnp.float32)
    slab_of = jnp.arange(N_SLAB * PAIRS_DEV, dtype=jnp.int32) // PAIRS_DEV
    target_cell = (slab_of[None, :] * CELL_DEV + pair_target).reshape(-1)
    source_cell = (slab_of[None, :] * CELL_DEV - HALO + pair_source).reshape(-1)
    inside = ((source_cell >= 0) & (source_cell < cell_seg)).astype(jnp.float32)
    source_clip = jnp.clip(source_cell, 0, cell_seg - 1).astype(jnp.int32)
    segment_of = jnp.broadcast_to(jnp.arange(N_SEG, dtype=jnp.int32)[:, None], pair_target.shape).reshape(-1)

    def fine_pair(target_pts, source_pts, source_den, weight_inside):
        strength = source_den.astype(jnp.float32) * quad_weights[None, :]
        return kernel_rows(target_pts.astype(jnp.float32), source_pts.astype(jnp.float32), strength) * weight_inside
    blocks = grouped(fine_pair, (positions[segment_of, target_cell], fine_points[segment_of, source_clip], fine_density[segment_of, source_clip], inside), 4)
    velocity = velocity.at[segment_of, target_cell].add(blocks)
    source_seg, slab_index, target_seg = jnp.meshgrid(jnp.arange(N_SEG, dtype=jnp.int32), jnp.arange(N_SLAB, dtype=jnp.int32), jnp.arange(N_SEG, dtype=jnp.int32), indexing='ij')
    junction_source = (slab_index * CELL_DEV + junction_cell).reshape(-1)
    junction_goal = (slab_index * CELL_DEV + junction_target[target_seg, slab_index, source_seg]).reshape(-1)
    alive_mask = (source_seg != target_seg).astype(jnp.float32).reshape(-1)
    source_seg = source_seg.reshape(-1)
    target_seg = target_seg.reshape(-1)

    def coarse_pair(target_pts, source_pts, source_den, weight_alive):
        strength = source_den.astype(jnp.float32) * coarse_weights[None, :]
        return kernel_rows(target_pts.astype(jnp.float32), source_pts.astype(jnp.float32), strength) * weight_alive
    junction_blocks = grouped(coarse_pair, (positions[target_seg, junction_goal], positions[source_seg, junction_source], density[source_seg, junction_source], alive_mask), 4)
    velocity = velocity.at[target_seg, junction_goal].add(junction_blocks)
    wall_seg = jnp.broadcast_to(jnp.arange(N_SEG, dtype=jnp.int32)[:, None, None], wall_near.shape).reshape(-1)
    wall_cell = jnp.broadcast_to(jnp.arange(cell_seg, dtype=jnp.int32)[None, :, None], wall_near.shape).reshape(-1)
    wall_patch = wall_near.reshape(-1)

    def wall_pair(target_pts, source_pts, source_den):
        return kernel_rows(target_pts.astype(jnp.float32), source_pts.astype(jnp.float32), source_den.astype(jnp.float32) * WALL_GAIN)
    wall_blocks = grouped(wall_pair, (positions[wall_seg, wall_cell], wall_points[wall_seg, wall_patch], wall_traction[wall_seg, wall_patch]), 4)
    velocity = velocity.at[wall_seg, wall_cell].add(wall_blocks)
    return velocity
```

```python
import functools
import math

import jax
import jax.numpy as jnp
from jax import lax
from jax.experimental import pallas as pl
from jax.experimental.pallas import tpu as pltpu
from jax.sharding import PartitionSpec as P

MESH = pl.DeviceIdType.MESH
HALO = 2
EPSILON2 = 0.05
WALL_GAIN = 3.0
LANES = 128
WIDE = 2 * LANES
TERMS = 16
SPLITS = 3
RAW = 6
F32 = jnp.float32
BF16 = jnp.bfloat16


def up(n, m):
    return -(-n // m) * m


def split(value, parts):
    out = []
    for _ in range(parts):
        piece = value.astype(BF16).astype(F32)
        out.append(piece)
        value = value - piece
    return out


def spread():
    shape = (3 * TERMS, RAW)
    r, c = (lax.broadcasted_iota(jnp.int32, shape, d) for d in range(2))

    def steps(first, count):
        return sum(jnp.where(r >= first + 3 * (k + 1), 1, 0) for k in range(count))

    at = jnp.where(
        r < 15, 3 + r - 3 * steps(0, 4), jnp.where(
            (r >= 19) & (r < 28), steps(19, 2), jnp.where(
                (r >= 28) & (r < 31), r - 28, jnp.where(
                    (r >= 32) & (r < 35), r - 32, jnp.where((r >= 40) & (r < 43), r - 37, -1)))))
    return jnp.where(c == at, jnp.where((r >= 32) & (r < 35), -2.0, 1.0), 0.0).astype(BF16)


def features(rep, weight):
    lanes = rep.shape[1]
    row = lax.broadcasted_iota(jnp.int32, (8, lanes), 0)
    y2, g = rep[32:40], rep[40:48]
    norm = 0.25 * jnp.sum(y2 * y2, axis=0, keepdims=True)
    dot = -0.5 * weight * jnp.sum(y2 * g, axis=0, keepdims=True)
    m = split(norm + EPSILON2, 3)
    first = jnp.where((row >= 3) & (row < 6), 1.0, y2)
    first = jnp.where(row == 6, m[0], jnp.where(row == 7, m[1], first))
    second = jnp.where(row == 0, m[2], 0.0)
    near = jnp.concatenate([first, second], axis=0).astype(BF16)
    one = rep[0:8] * weight * jnp.where(row < 3, 1.0, rep[16:24])
    two = rep[8:16] * weight * jnp.where(row >= 4, norm, rep[24:32])
    two = two + jnp.where(row >= 4, dot * rep[24:32], 0.0)
    parts = split(jnp.concatenate([one, two], axis=0), SPLITS)
    return near, jnp.concatenate(parts, axis=0).astype(BF16)


def kernel(
    cfg,
    pair_target_far, pair_source_far, junction_cell_far, junction_target_far, wall_near_far,
    positions, density, upsample, quad_far, coarse_far, wall_points, wall_traction,
    out,
    pair_target, pair_source, junction_cell, junction_target, wall_near, quad, coarse,
    own, mine, cells, jsend, jrecv, wall_own, walls, ups, rows, quad_row, coarse_row, tail, xt, xs,
    local_sem, halo_send, halo_recv, junction_send, junction_recv, wall_send, wall_recv,
):
    count, points, fine_points, pairs, near, patch, segs, slabs, per_slab = cfg
    pt = xs.shape[2]
    rows_t = xt.shape[1]
    seg, slab = lax.axis_index("seg"), lax.axis_index("slab")

    barrier = pltpu.get_barrier_semaphore()
    for o in range(1, segs):
        pl.semaphore_signal(barrier, inc=1, device_id={"seg": lax.rem(seg + o, segs)}, device_id_type=MESH)
    for o in range(1, slabs):
        pl.semaphore_signal(barrier, inc=1, device_id={"slab": lax.rem(slab + o, slabs)}, device_id_type=MESH)

    copies = [
        pltpu.make_async_copy(positions.at[0], own.at[0], local_sem.at[0]),
        pltpu.make_async_copy(density.at[0], own.at[1], local_sem.at[1]),
        pltpu.make_async_copy(wall_points.at[0], wall_own.at[0], local_sem.at[2]),
        pltpu.make_async_copy(wall_traction.at[0], wall_own.at[1], local_sem.at[3]),
    ]
    big = pltpu.make_async_copy(upsample, ups, local_sem.at[4])
    tables = [
        pltpu.make_async_copy(source, target, local_sem.at[5 + i]) for i, (source, target) in enumerate([
            (pair_target_far, pair_target), (pair_source_far, pair_source), (junction_cell_far, junction_cell),
            (junction_target_far, junction_target), (wall_near_far, wall_near), (quad_far, quad), (coarse_far, coarse)])
    ]
    for copy in copies + tables:
        copy.start()
    big.start()
    for copy in copies + tables:
        copy.wait()

    mine[...] = jnp.zeros_like(mine)

    @pl.when(slab == 0)
    def _():
        cells[0:HALO] = jnp.zeros((HALO, RAW, pt), BF16)

    @pl.when(slab == slabs - 1)
    def _():
        cells[HALO + count:] = jnp.zeros((HALO, RAW, pt), BF16)

    coords = [own[0, i].astype(F32) for i in range(3)]
    loads = [own[1, i].astype(F32) for i in range(3)]
    for c in range(count):
        mine[c, :, 0:points] = jnp.concatenate(
            [line[c:c + 1] for line in coords + loads], axis=0).astype(BF16)
    cells[HALO:HALO + count] = mine[...]
    for b in range(segs):
        jsend[b] = mine[junction_cell[0, 0, b]]
    for p in range(per_slab):
        walls[slab * per_slab + p] = jnp.concatenate(
            [wall_own[0, p].astype(F32), wall_own[1, p].astype(F32)], axis=0).astype(BF16)
    pl.semaphore_wait(barrier, segs - 1 + slabs - 1)

    def halo_up():
        return pltpu.make_async_remote_copy(
            cells.at[pl.ds(count, HALO)], cells.at[pl.ds(0, HALO)], halo_send.at[0], halo_recv.at[0],
            device_id={"slab": lax.rem(slab + 1, slabs)}, device_id_type=MESH)

    def halo_down():
        return pltpu.make_async_remote_copy(
            cells.at[pl.ds(HALO, HALO)], cells.at[pl.ds(HALO + count, HALO)], halo_send.at[1], halo_recv.at[1],
            device_id={"slab": lax.rem(slab + slabs - 1, slabs)}, device_id_type=MESH)

    def junction(o):
        return pltpu.make_async_remote_copy(
            jsend.at[lax.rem(seg + o, segs)], jrecv.at[seg], junction_send.at[o], junction_recv.at[o],
            device_id={"seg": lax.rem(seg + o, segs)}, device_id_type=MESH)

    def junction_in(o):
        return pltpu.make_async_remote_copy(
            jsend.at[seg], jrecv.at[lax.rem(seg + segs - o, segs)], junction_send.at[o], junction_recv.at[o],
            device_id={"seg": lax.rem(seg + o, segs)}, device_id_type=MESH)

    def wall(o, of):
        slot = pl.ds(of * per_slab, per_slab)
        return pltpu.make_async_remote_copy(
            walls.at[slot], walls.at[slot], wall_send.at[o], wall_recv.at[o],
            device_id={"slab": lax.rem(slab + o, slabs)}, device_id_type=MESH)

    @pl.when(slab < slabs - 1)
    def _():
        halo_up().start()

    @pl.when(slab > 0)
    def _():
        halo_down().start()

    for o in range(1, segs):
        junction(o).start()
    for o in range(slabs - 1, 0, -1):
        wall(o, slab).start()

    chosen = spread()
    quad_row[...] = jnp.zeros_like(quad_row)
    coarse_row[...] = jnp.zeros_like(coarse_row)
    quad_row[:, 0:fine_points] = quad[...][None]
    coarse_row[:, 0:points] = coarse[...][None]
    tail[...] = jnp.zeros_like(tail)
    rows[...] = jnp.zeros_like(rows)
    xs[...] = jnp.zeros_like(xs)
    norms = split(coords[0] * coords[0] + coords[1] * coords[1] + coords[2] * coords[2], 3)
    rows[6:9] = jnp.ones((3, pt), F32)
    for c in range(count):
        for i in range(3):
            xs[c, i:i + 1, 0:points] = coords[i][c:c + 1]
            rows[i:i + 1, 0:points] = coords[i][c:c + 1]
            rows[3 + i:4 + i, 0:points] = norms[i][c:c + 1]
        xt[c] = rows[...].T[0:rows_t].astype(BF16)

    def repeat(raw):
        return jnp.dot(chosen, raw, preferred_element_type=F32)

    def distance(target, near_rows):
        return jnp.dot(xt[target], near_rows, preferred_element_type=F32)

    def weigh(value):
        inverse = lax.rsqrt(value)
        return (inverse * inverse * inverse).astype(BF16)

    def reduce(weights, value):
        sums = lax.dot_general(weights, value, (((1,), (1,)), ((), ())), preferred_element_type=F32)
        return sums[0:TERMS] + sums[TERMS:2 * TERMS] + sums[2 * TERMS:3 * TERMS]

    totals = {}

    def run(units):
        held = []
        for k in range(0, len(units) + 2, 2):
            fresh = []
            for item, target, make in units[k:k + 2]:
                near_rows, weights = features(*make())
                fresh.append((item, weights, distance(target, near_rows)))
            sums = [(item, reduce(weights, value)) for item, weights, value in held]
            held = [(item, weights, weigh(value)) for item, weights, value in fresh]
            for item, value in sums:
                totals[item] = totals[item] + value if item in totals else value

    @pl.when(slab > 0)
    def _():
        halo_up().wait_recv()

    @pl.when(slab < slabs - 1)
    def _():
        halo_down().wait_recv()

    big.wait()
    lhs = jnp.concatenate([repeat(cells[pair_source[0, k]]) for k in range(pairs)], axis=0)[:, 0:points].astype(BF16)

    def fine(start):
        stop = min(start + WIDE, fine_points)
        value = jnp.dot(lhs, ups[:, start:stop], preferred_element_type=F32)
        if stop - start < WIDE:
            tail[:, 0:stop - start] = value
            value = tail[:, 0:up(stop - start, LANES)]
        return value.astype(BF16).astype(F32)

    units = []
    for start in range(0, fine_points, WIDE):
        cache = []

        def make(k, start=start, cache=cache):
            if not cache:
                cache.append(fine(start))
            value = cache[0][3 * TERMS * k:3 * TERMS * (k + 1)]
            return value, quad_row[:, start:start + value.shape[1]]

        units += [(("pair", k), pair_target[0, k], functools.partial(make, k)) for k in range(pairs)]
    run(units)

    for o in range(1, segs):
        junction_in(o).wait_recv()
    units = []
    for start in range(0, pt, WIDE):
        for o in range(1, segs):
            def make(start=start, o=o):
                at = slice(start, min(start + WIDE, pt))
                return repeat(jrecv[lax.rem(seg + segs - o, segs), :, at]), coarse_row[:, at]

            units.append((("junction", o), junction_target[0, 0, lax.rem(seg + segs - o, segs)], make))
    run(units)

    for o in range(1, slabs):
        wall(o, lax.rem(slab + slabs - o, slabs)).wait_recv()
    units = []
    for c in range(count):
        def make(c=c):
            value = repeat(jnp.concatenate([walls[wall_near[0, n, c]] for n in range(near)], axis=1))
            return value, WALL_GAIN

        units.append((("wall", c), c, make))
    run(units)

    places = [(("pair", k), pair_target[0, k]) for k in range(pairs)]
    places += [(("junction", o), junction_target[0, 0, lax.rem(seg + segs - o, segs)]) for o in range(1, segs)]
    for c in range(count):
        total = totals["wall", c]
        for item, target in places:
            total = total + jnp.where(target == c, 1.0, 0.0) * totals[item]
        total = total[:, 0:points]
        x = xs[c, :, 0:points]
        x = [x[i:i + 1] for i in range(3)]
        a, b, h = total[0:3], [total[3 + 3 * i:6 + 3 * i] for i in range(3)], total[12:15]
        square = x[0] * x[0] + x[1] * x[1] + x[2] * x[2] + 2.0 * EPSILON2
        value = square * a + h - 2.0 * (x[0] * b[0] + x[1] * b[1] + x[2] * b[2])
        trace = b[0][0:1] + b[1][1:2] + b[2][2:3]
        lift = x[0] * a[0:1] + x[1] * a[1:2] + x[2] * a[2:3] - trace
        for i in range(3):
            along = x[0] * b[i][0:1] + x[1] * b[i][1:2] + x[2] * b[i][2:3]
            out[0, i, c:c + 1] = (value[i:i + 1] + x[i] * lift - along) * (1.0 / (8.0 * math.pi))

    @pl.when(slab < slabs - 1)
    def _():
        halo_up().wait_send()

    @pl.when(slab > 0)
    def _():
        halo_down().wait_send()

    for o in range(1, segs):
        junction(o).wait_send()
    for o in range(1, slabs):
        wall(o, slab).wait_send()


def local(segs, slabs, positions, density, upsample, quad_weights, coarse_weights, pair_target, pair_source,
          junction_cell, junction_target, wall_points, wall_traction, wall_near):
    count, points = positions.shape[1], positions.shape[3]
    turned = (1, 3, count, points)
    fine_points = upsample.shape[1]
    pairs, near = pair_target.shape[1], wall_near.shape[2]
    per_slab, patch = wall_points.shape[1], wall_points.shape[3]
    cfg = (count, points, fine_points, pairs, near, patch, segs, slabs, per_slab)
    pt = up(points, LANES)
    vmem = pl.BlockSpec(memory_space=pltpu.VMEM)
    far = pl.BlockSpec(memory_space=pl.ANY)
    dma = pltpu.SemaphoreType.DMA
    result = pl.pallas_call(
        functools.partial(kernel, cfg),
        out_shape=jax.ShapeDtypeStruct(turned, F32),
        in_specs=[far] * 12,
        out_specs=vmem,
        scratch_shapes=[
            pltpu.SMEM(pair_target.shape, jnp.int32),
            pltpu.SMEM(pair_source.shape, jnp.int32),
            pltpu.SMEM(junction_cell.shape, jnp.int32),
            pltpu.SMEM(junction_target.shape, jnp.int32),
            pltpu.SMEM((1, near, count), jnp.int32),
            pltpu.VMEM(quad_weights.shape, F32),
            pltpu.VMEM(coarse_weights.shape, F32),
            pltpu.VMEM((2,) + turned[1:], BF16),
            pltpu.VMEM((count, RAW, pt), BF16),
            pltpu.VMEM((count + 2 * HALO, RAW, pt), BF16),
            pltpu.VMEM((segs, RAW, pt), BF16),
            pltpu.VMEM((segs, RAW, pt), BF16),
            pltpu.VMEM((2, per_slab, 3, patch), BF16),
            pltpu.VMEM((slabs * per_slab, RAW, patch), BF16),
            pltpu.VMEM(upsample.shape, BF16),
            pltpu.VMEM((TERMS, pt), F32),
            pltpu.VMEM((1, up(fine_points, LANES)), F32),
            pltpu.VMEM((1, pt), F32),
            pltpu.VMEM((3 * TERMS * pairs, WIDE), F32),
            pltpu.VMEM((count, up(points, 16), TERMS), BF16),
            pltpu.VMEM((count, 3, pt), F32),
            dma((12,)), dma((2,)), dma((2,)), dma((segs,)), dma((segs,)), dma((slabs,)), dma((slabs,)),
        ],
        compiler_params=pltpu.CompilerParams(collective_id=0, has_side_effects=True),
    )(pair_target, pair_source, junction_cell, junction_target, wall_near.transpose(0, 2, 1),
      positions.transpose(0, 2, 1, 3), density.transpose(0, 2, 1, 3), upsample, quad_weights, coarse_weights,
      wall_points, wall_traction)
    return result.transpose(0, 2, 1, 3)


def solution(mesh):
    placed = (
        P("seg", "slab", None, None),
        P("seg", "slab", None, None),
        P(),
        P(),
        P(),
        P("seg", "slab"),
        P("seg", "slab"),
        P("seg", "slab", None),
        P("seg", "slab", None),
        P("seg", "slab", None, None),
        P("seg", "slab", None, None),
        P("seg", "slab", None),
    )
    body = functools.partial(local, mesh.shape["seg"], mesh.shape["slab"])
    return jax.shard_map(
        body, mesh=mesh, in_specs=placed, out_specs=P("seg", "slab", None, None), check_vma=False
    )
```

```python
import functools
import math

import jax
import jax.numpy as jnp
from jax import lax
from jax.experimental import pallas as pl
from jax.experimental.pallas import tpu as pltpu
from jax.sharding import PartitionSpec as P

MESH = pl.DeviceIdType.MESH
HALO = 2
EPSILON2 = 0.05
WALL_GAIN = 3.0
LANES = 128
WIDE = 2 * LANES
TERMS = 16
SPLITS = 3
RAW = 6
F32 = jnp.float32
BF16 = jnp.bfloat16


def up(n, m):
    return -(-n // m) * m


def split(value, parts):
    out = []
    for _ in range(parts):
        piece = value.astype(BF16).astype(F32)
        out.append(piece)
        value = value - piece
    return out


def spread():
    shape = (3 * TERMS, RAW)
    r, c = (lax.broadcasted_iota(jnp.int32, shape, d) for d in range(2))

    def steps(first, count):
        return sum(jnp.where(r >= first + 3 * (k + 1), 1, 0) for k in range(count))

    at = jnp.where(
        r < 15, 3 + r - 3 * steps(0, 4), jnp.where(
            (r >= 19) & (r < 28), steps(19, 2), jnp.where(
                (r >= 28) & (r < 31), r - 28, jnp.where(
                    (r >= 32) & (r < 35), r - 32, jnp.where((r >= 40) & (r < 43), r - 37, -1)))))
    return jnp.where(c == at, jnp.where((r >= 32) & (r < 35), -2.0, 1.0), 0.0).astype(BF16)


def features(rep, weight):
    lanes = rep.shape[1]
    row = lax.broadcasted_iota(jnp.int32, (8, lanes), 0)
    y2, g = rep[32:40], rep[40:48]
    norm = 0.25 * jnp.sum(y2 * y2, axis=0, keepdims=True)
    dot = -0.5 * weight * jnp.sum(y2 * g, axis=0, keepdims=True)
    m = split(norm + EPSILON2, 3)
    first = jnp.where((row >= 3) & (row < 6), 1.0, y2)
    first = jnp.where(row == 6, m[0], jnp.where(row == 7, m[1], first))
    second = jnp.where(row == 0, m[2], 0.0)
    near = jnp.concatenate([first, second], axis=0).astype(BF16)
    one = rep[0:8] * weight * jnp.where(row < 3, 1.0, rep[16:24])
    two = rep[8:16] * weight * jnp.where(row >= 4, norm, rep[24:32])
    two = two + jnp.where(row >= 4, dot * rep[24:32], 0.0)
    parts = split(jnp.concatenate([one, two], axis=0), SPLITS)
    return near, jnp.concatenate(parts, axis=0).astype(BF16)


def kernel(
    cfg,
    pair_target_far, pair_source_far, junction_cell_far, junction_target_far, wall_near_far,
    positions, density, upsample, quad_far, coarse_far, wall_points, wall_traction,
    out,
    pair_target, pair_source, junction_cell, junction_target, wall_near, quad, coarse,
    own, mine, cells, jsend, jrecv, wall_own, walls, ups, rows, quad_row, coarse_row, tail, xt, xs,
    local_sem, halo_send, halo_recv, junction_send, junction_recv, wall_send, wall_recv,
):
    count, points, fine_points, pairs, near, patch, segs, slabs, per_slab = cfg
    pt = xs.shape[2]
    rows_t = xt.shape[1]
    seg, slab = lax.axis_index("seg"), lax.axis_index("slab")

    barrier = pltpu.get_barrier_semaphore()
    for o in range(1, segs):
        pl.semaphore_signal(barrier, inc=1, device_id={"seg": lax.rem(seg + o, segs)}, device_id_type=MESH)
    for o in range(1, slabs):
        pl.semaphore_signal(barrier, inc=1, device_id={"slab": lax.rem(slab + o, slabs)}, device_id_type=MESH)

    copies = [
        pltpu.make_async_copy(positions.at[0], own.at[0], local_sem.at[0]),
        pltpu.make_async_copy(density.at[0], own.at[1], local_sem.at[1]),
        pltpu.make_async_copy(wall_points.at[0], wall_own.at[0], local_sem.at[2]),
        pltpu.make_async_copy(wall_traction.at[0], wall_own.at[1], local_sem.at[3]),
    ]
    big = pltpu.make_async_copy(upsample, ups, local_sem.at[4])
    tables = [
        pltpu.make_async_copy(source, target, local_sem.at[5 + i]) for i, (source, target) in enumerate([
            (pair_target_far, pair_target), (pair_source_far, pair_source), (junction_cell_far, junction_cell),
            (junction_target_far, junction_target), (wall_near_far, wall_near), (quad_far, quad), (coarse_far, coarse)])
    ]
    for copy in copies + tables:
        copy.start()
    big.start()
    for copy in copies + tables:
        copy.wait()

    mine[...] = jnp.zeros_like(mine)

    @pl.when(slab == 0)
    def _():
        cells[0:HALO] = jnp.zeros((HALO, RAW, pt), BF16)

    @pl.when(slab == slabs - 1)
    def _():
        cells[HALO + count:] = jnp.zeros((HALO, RAW, pt), BF16)

    coords = [own[0, i].astype(F32) for i in range(3)]
    loads = [own[1, i].astype(F32) for i in range(3)]
    for c in range(count):
        mine[c, :, 0:points] = jnp.concatenate(
            [line[c:c + 1] for line in coords + loads], axis=0).astype(BF16)
    cells[HALO:HALO + count] = mine[...]
    for b in range(segs):
        jsend[b] = mine[junction_cell[0, 0, b]]
    for p in range(per_slab):
        walls[slab * per_slab + p] = jnp.concatenate(
            [wall_own[0, p].astype(F32), wall_own[1, p].astype(F32)], axis=0).astype(BF16)
    pl.semaphore_wait(barrier, segs - 1 + slabs - 1)

    def halo_up():
        return pltpu.make_async_remote_copy(
            cells.at[pl.ds(count, HALO)], cells.at[pl.ds(0, HALO)], halo_send.at[0], halo_recv.at[0],
            device_id={"slab": lax.rem(slab + 1, slabs)}, device_id_type=MESH)

    def halo_down():
        return pltpu.make_async_remote_copy(
            cells.at[pl.ds(HALO, HALO)], cells.at[pl.ds(HALO + count, HALO)], halo_send.at[1], halo_recv.at[1],
            device_id={"slab": lax.rem(slab + slabs - 1, slabs)}, device_id_type=MESH)

    def junction(o):
        return pltpu.make_async_remote_copy(
            jsend.at[lax.rem(seg + o, segs)], jrecv.at[seg], junction_send.at[o], junction_recv.at[o],
            device_id={"seg": lax.rem(seg + o, segs)}, device_id_type=MESH)

    def junction_in(o):
        return pltpu.make_async_remote_copy(
            jsend.at[seg], jrecv.at[lax.rem(seg + segs - o, segs)], junction_send.at[o], junction_recv.at[o],
            device_id={"seg": lax.rem(seg + o, segs)}, device_id_type=MESH)

    def wall(o, of):
        slot = pl.ds(of * per_slab, per_slab)
        return pltpu.make_async_remote_copy(
            walls.at[slot], walls.at[slot], wall_send.at[o], wall_recv.at[o],
            device_id={"slab": lax.rem(slab + o, slabs)}, device_id_type=MESH)

    @pl.when(slab < slabs - 1)
    def _():
        halo_up().start()

    @pl.when(slab > 0)
    def _():
        halo_down().start()

    for o in range(1, segs):
        junction(o).start()
    for o in range(slabs - 1, 0, -1):
        wall(o, slab).start()

    chosen = spread()
    quad_row[...] = jnp.zeros_like(quad_row)
    coarse_row[...] = jnp.zeros_like(coarse_row)
    quad_row[:, 0:fine_points] = quad[...][None]
    coarse_row[:, 0:points] = coarse[...][None]
    tail[...] = jnp.zeros_like(tail)
    rows[...] = jnp.zeros_like(rows)
    xs[...] = jnp.zeros_like(xs)
    norms = split(coords[0] * coords[0] + coords[1] * coords[1] + coords[2] * coords[2], 3)
    rows[6:9] = jnp.ones((3, pt), F32)
    for c in range(count):
        for i in range(3):
            xs[c, i:i + 1, 0:points] = coords[i][c:c + 1]
            rows[i:i + 1, 0:points] = coords[i][c:c + 1]
            rows[3 + i:4 + i, 0:points] = norms[i][c:c + 1]
        xt[c] = rows[...].T[0:rows_t].astype(BF16)

    def repeat(raw):
        return jnp.dot(chosen, raw, preferred_element_type=F32)

    def distance(target, near_rows):
        return jnp.dot(xt[target], near_rows, preferred_element_type=F32)

    def weigh(value):
        inverse = lax.rsqrt(value)
        return (inverse * inverse * inverse).astype(BF16)

    def reduce(weights, value):
        sums = lax.dot_general(weights, value, (((1,), (1,)), ((), ())), preferred_element_type=F32)
        return sums[0:TERMS] + sums[TERMS:2 * TERMS] + sums[2 * TERMS:3 * TERMS]

    totals = {}

    def run(units):
        held = []
        for k in range(0, len(units) + 2, 2):
            fresh = []
            for item, target, make in units[k:k + 2]:
                near_rows, weights = features(*make())
                fresh.append((item, weights, distance(target, near_rows)))
            sums = [(item, reduce(weights, value)) for item, weights, value in held]
            held = [(item, weights, weigh(value)) for item, weights, value in fresh]
            for item, value in sums:
                totals[item] = totals[item] + value if item in totals else value

    @pl.when(slab > 0)
    def _():
        halo_up().wait_recv()

    @pl.when(slab < slabs - 1)
    def _():
        halo_down().wait_recv()

    big.wait()
    lhs = jnp.concatenate([repeat(cells[pair_source[0, k]]) for k in range(pairs)], axis=0)[:, 0:points].astype(BF16)

    def fine(start):
        stop = min(start + WIDE, fine_points)
        value = jnp.dot(lhs, ups[:, start:stop], preferred_element_type=F32)
        if stop - start < WIDE:
            tail[:, 0:stop - start] = value
            value = tail[:, 0:up(stop - start, LANES)]
        return value.astype(BF16).astype(F32)

    units = []
    for start in range(0, fine_points, WIDE):
        cache = []

        def make(k, start=start, cache=cache):
            if not cache:
                cache.append(fine(start))
            value = cache[0][3 * TERMS * k:3 * TERMS * (k + 1)]
            return value, quad_row[:, start:start + value.shape[1]]

        units += [(("pair", k), pair_target[0, k], functools.partial(make, k)) for k in range(pairs)]
    run(units)

    for o in range(1, segs):
        junction_in(o).wait_recv()
    units = []
    for start in range(0, pt, WIDE):
        for o in range(1, segs):
            def make(start=start, o=o):
                at = slice(start, min(start + WIDE, pt))
                return repeat(jrecv[lax.rem(seg + segs - o, segs), :, at]), coarse_row[:, at]

            units.append((("junction", o), junction_target[0, 0, lax.rem(seg + segs - o, segs)], make))
    run(units)

    for o in range(1, slabs):
        wall(o, lax.rem(slab + slabs - o, slabs)).wait_recv()
    units = []
    for c in range(count):
        def make(c=c):
            value = repeat(jnp.concatenate([walls[wall_near[0, n, c]] for n in range(near)], axis=1))
            return value, WALL_GAIN

        units.append((("wall", c), c, make))
    run(units)

    places = [(("pair", k), pair_target[0, k]) for k in range(pairs)]
    places += [(("junction", o), junction_target[0, 0, lax.rem(seg + segs - o, segs)]) for o in range(1, segs)]
    for c in range(count):
        total = totals["wall", c]
        for item, target in places:
            total = total + jnp.where(target == c, 1.0, 0.0) * totals[item]
        total = total[:, 0:points]
        x = xs[c, :, 0:points]
        x = [x[i:i + 1] for i in range(3)]
        a, b, h = total[0:3], [total[3 + 3 * i:6 + 3 * i] for i in range(3)], total[12:15]
        square = x[0] * x[0] + x[1] * x[1] + x[2] * x[2] + 2.0 * EPSILON2
        value = square * a + h - 2.0 * (x[0] * b[0] + x[1] * b[1] + x[2] * b[2])
        trace = b[0][0:1] + b[1][1:2] + b[2][2:3]
        lift = x[0] * a[0:1] + x[1] * a[1:2] + x[2] * a[2:3] - trace
        for i in range(3):
            along = x[0] * b[i][0:1] + x[1] * b[i][1:2] + x[2] * b[i][2:3]
            out[0, i, c:c + 1] = (value[i:i + 1] + x[i] * lift - along) * (1.0 / (8.0 * math.pi))

    @pl.when(slab < slabs - 1)
    def _():
        halo_up().wait_send()

    @pl.when(slab > 0)
    def _():
        halo_down().wait_send()

    for o in range(1, segs):
        junction(o).wait_send()
    for o in range(1, slabs):
        wall(o, slab).wait_send()


def local(segs, slabs, positions, density, upsample, quad_weights, coarse_weights, pair_target, pair_source,
          junction_cell, junction_target, wall_points, wall_traction, wall_near):
    count, points = positions.shape[1], positions.shape[3]
    turned = (1, 3, count, points)
    fine_points = upsample.shape[1]
    pairs, near = pair_target.shape[1], wall_near.shape[2]
    per_slab, patch = wall_points.shape[1], wall_points.shape[3]
    cfg = (count, points, fine_points, pairs, near, patch, segs, slabs, per_slab)
    pt = up(points, LANES)
    vmem = pl.BlockSpec(memory_space=pltpu.VMEM)
    far = pl.BlockSpec(memory_space=pl.ANY)
    dma = pltpu.SemaphoreType.DMA
    result = pl.pallas_call(
        functools.partial(kernel, cfg),
        out_shape=pltpu.VMEM(turned, F32),
        in_specs=[far] * 12,
        out_specs=vmem,
        scratch_shapes=[
            pltpu.SMEM(pair_target.shape, jnp.int32),
            pltpu.SMEM(pair_source.shape, jnp.int32),
            pltpu.SMEM(junction_cell.shape, jnp.int32),
            pltpu.SMEM(junction_target.shape, jnp.int32),
            pltpu.SMEM((1, near, count), jnp.int32),
            pltpu.VMEM(quad_weights.shape, F32),
            pltpu.VMEM(coarse_weights.shape, F32),
            pltpu.VMEM((2,) + turned[1:], BF16),
            pltpu.VMEM((count, RAW, pt), BF16),
            pltpu.VMEM((count + 2 * HALO, RAW, pt), BF16),
            pltpu.VMEM((segs, RAW, pt), BF16),
            pltpu.VMEM((segs, RAW, pt), BF16),
            pltpu.VMEM((2, per_slab, 3, patch), BF16),
            pltpu.VMEM((slabs * per_slab, RAW, patch), BF16),
            pltpu.VMEM(upsample.shape, BF16),
            pltpu.VMEM((TERMS, pt), F32),
            pltpu.VMEM((1, up(fine_points, LANES)), F32),
            pltpu.VMEM((1, pt), F32),
            pltpu.VMEM((3 * TERMS * pairs, WIDE), F32),
            pltpu.VMEM((count, up(points, 16), TERMS), BF16),
            pltpu.VMEM((count, 3, pt), F32),
            dma((12,)), dma((2,)), dma((2,)), dma((segs,)), dma((segs,)), dma((slabs,)), dma((slabs,)),
        ],
        compiler_params=pltpu.CompilerParams(collective_id=0, has_side_effects=True),
    )(pair_target, pair_source, junction_cell, junction_target, wall_near.transpose(0, 2, 1),
      positions.transpose(0, 2, 1, 3), density.transpose(0, 2, 1, 3), upsample, quad_weights, coarse_weights,
      wall_points, wall_traction)
    return result.transpose(0, 2, 1, 3)


def solution(mesh):
    placed = (
        P("seg", "slab", None, None),
        P("seg", "slab", None, None),
        P(),
        P(),
        P(),
        P("seg", "slab"),
        P("seg", "slab"),
        P("seg", "slab", None),
        P("seg", "slab", None),
        P("seg", "slab", None, None),
        P("seg", "slab", None, None),
        P("seg", "slab", None),
    )
    body = functools.partial(local, mesh.shape["seg"], mesh.shape["slab"])
    return jax.shard_map(
        body, mesh=mesh, in_specs=placed, out_specs=P("seg", "slab", None, None), check_vma=False
    )
```

```python
import functools
import math

import jax
import jax.numpy as jnp
from jax import lax
from jax.experimental import pallas as pl
from jax.experimental.pallas import tpu as pltpu
from jax.sharding import PartitionSpec as P

MESH = pl.DeviceIdType.MESH
HALO = 2
EPSILON2 = 0.05
WALL_GAIN = 3.0
LANES = 128
WIDE = 2 * LANES
TERMS = 16
SPLITS = 3
RAW = 6
CORES = 2
RELAY = 3
RELAY_STEP = 4
F32 = jnp.float32
BF16 = jnp.bfloat16


def up(n, m):
    return -(-n // m) * m


def grid(n):
    columns = max(k for k in range(1, n + 1) if n % k == 0 and k * k <= n)
    return n // columns, columns


def split(value, parts):
    out = []
    for _ in range(parts):
        piece = value.astype(BF16).astype(F32)
        out.append(piece)
        value = value - piece
    return out


def spread():
    shape = (3 * TERMS, RAW)
    r, c = (lax.broadcasted_iota(jnp.int32, shape, d) for d in range(2))

    def steps(first, count):
        return sum(jnp.where(r >= first + 3 * (k + 1), 1, 0) for k in range(count))

    at = jnp.where(
        r < 15, 3 + r - 3 * steps(0, 4), jnp.where(
            (r >= 19) & (r < 28), steps(19, 2), jnp.where(
                (r >= 28) & (r < 31), r - 28, jnp.where(
                    (r >= 32) & (r < 35), r - 32, jnp.where((r >= 40) & (r < 43), r - 37, -1)))))
    return jnp.where(c == at, jnp.where((r >= 32) & (r < 35), -2.0, 1.0), 0.0).astype(BF16)


def features(rep, weight):
    lanes = rep.shape[1]
    row = lax.broadcasted_iota(jnp.int32, (8, lanes), 0)
    y2, g = rep[32:40], rep[40:48]
    norm = 0.25 * jnp.sum(y2 * y2, axis=0, keepdims=True)
    dot = -0.5 * weight * jnp.sum(y2 * g, axis=0, keepdims=True)
    m = split(norm + EPSILON2, 3)
    first = jnp.where((row >= 3) & (row < 6), 1.0, y2)
    first = jnp.where(row == 6, m[0], jnp.where(row == 7, m[1], first))
    second = jnp.where(row == 0, m[2], 0.0)
    near = jnp.concatenate([first, second], axis=0).astype(BF16)
    one = rep[0:8] * weight * jnp.where(row < 3, 1.0, rep[16:24])
    two = rep[8:16] * weight * jnp.where(row >= 4, norm, rep[24:32])
    two = two + jnp.where(row >= 4, dot * rep[24:32], 0.0)
    parts = split(jnp.concatenate([one, two], axis=0), SPLITS)
    return near, jnp.concatenate(parts, axis=0).astype(BF16)


def kernel(
    cfg,
    pair_target_far, pair_source_far, junction_cell_far, junction_target_far, wall_near_far,
    positions, density, upsample, quad_far, coarse_far, wall_points, wall_traction,
    out,
    pair_target, pair_source, junction_cell, junction_target, wall_near, quad, coarse,
    own, mine, cells, jsend, mid, jrecv, wall_own, walls, ups, rows, quad_row, coarse_row, tail, xt, xs,
    local_sem, halo_send, halo_recv, junction_send, junction_recv, wall_send, wall_recv, up_send, up_recv, down_send, down_recv,
):
    count, points, fine_points, pairs, near, patch, segs, slabs, per_slab = cfg
    pt = xs.shape[2]
    rows_t = xt.shape[1]
    seg, slab = lax.axis_index("seg"), lax.axis_index("slab")
    lines, columns = grid(segs)
    levels = slabs // CORES
    line, column = lax.div(seg, columns), lax.rem(seg, columns)
    level, core = lax.div(slab, CORES), lax.rem(slab, CORES)
    partner = slab + 1 - 2 * core
    above, below = level < levels - 1, level > 0

    def turn(base, o, size):
        return lax.rem(base + (o + size), size)

    def across(dy, dx):
        return {"seg": turn(line, dy, lines) * columns + turn(column, dx, columns)}

    barrier = pltpu.get_barrier_semaphore()

    def greet(device):
        pl.semaphore_signal(barrier, inc=1, device_id=device, device_id_type=MESH)

    @pl.when(above)
    def _():
        greet({"slab": slab + CORES})

    @pl.when(below)
    def _():
        greet({"slab": slab - CORES})

    @pl.when((core == 1) & above)
    def _():
        greet({"slab": slab + 1})

    @pl.when((core == 0) & below)
    def _():
        greet({"slab": slab - 1})

    for dx in range(1, columns):
        greet(across(0, dx))
    for dy in range(1, lines):
        greet(across(dy, 0))
    greet({"slab": partner})

    copies = [
        pltpu.make_async_copy(positions.at[0], own.at[0], local_sem.at[0]),
        pltpu.make_async_copy(density.at[0], own.at[1], local_sem.at[1]),
        pltpu.make_async_copy(wall_points.at[0], wall_own.at[0], local_sem.at[2]),
        pltpu.make_async_copy(wall_traction.at[0], wall_own.at[1], local_sem.at[3]),
    ]
    big = pltpu.make_async_copy(upsample, ups, local_sem.at[4])
    tables = [
        pltpu.make_async_copy(source, target, local_sem.at[5 + i]) for i, (source, target) in enumerate([
            (pair_target_far, pair_target), (pair_source_far, pair_source), (junction_cell_far, junction_cell),
            (junction_target_far, junction_target), (wall_near_far, wall_near), (quad_far, quad), (coarse_far, coarse)])
    ]
    for copy in copies + tables:
        copy.start()
    big.start()
    for copy in copies + tables:
        copy.wait()

    mine[...] = jnp.zeros_like(mine)

    @pl.when(slab == 0)
    def _():
        cells[0:HALO] = jnp.zeros((HALO, RAW, pt), BF16)

    @pl.when(slab == slabs - 1)
    def _():
        cells[HALO + count:] = jnp.zeros((HALO, RAW, pt), BF16)

    coords = [own[0, i].astype(F32) for i in range(3)]
    loads = [own[1, i].astype(F32) for i in range(3)]
    for c in range(count):
        mine[c, :, 0:points] = jnp.concatenate(
            [line[c:c + 1] for line in coords + loads], axis=0).astype(BF16)
    cells[HALO:HALO + count] = mine[...]
    for b in range(segs):
        jsend[b % columns, b // columns] = mine[junction_cell[0, 0, b]]
    for p in range(per_slab):
        walls[slab * per_slab + p] = jnp.concatenate(
            [wall_own[0, p].astype(F32), wall_own[1, p].astype(F32)], axis=0).astype(BF16)
    beside = jnp.where(above, 1, 0) + jnp.where(below, 1, 0) + jnp.where(core == 1, jnp.where(above, 1, 0), jnp.where(below, 1, 0))
    pl.semaphore_wait(barrier, lines - 1 + columns - 1 + 1 + beside)

    def halo_up():
        return pltpu.make_async_remote_copy(
            cells.at[pl.ds(count, HALO)], cells.at[pl.ds(0, HALO)], halo_send.at[0], halo_recv.at[0],
            device_id={"slab": lax.rem(slab + 1, slabs)}, device_id_type=MESH)

    def halo_down():
        return pltpu.make_async_remote_copy(
            cells.at[pl.ds(HALO, HALO)], cells.at[pl.ds(HALO + count, HALO)], halo_send.at[1], halo_recv.at[1],
            device_id={"slab": lax.rem(slab + slabs - 1, slabs)}, device_id_type=MESH)

    def junction(dy, dx):
        i = dy * columns + dx
        sems = junction_send.at[i], junction_recv.at[i]
        if dy == 0:
            return pltpu.make_async_remote_copy(
                jsend.at[turn(column, dx, columns)], mid.at[:, column], *sems,
                device_id=across(0, dx), device_id_type=MESH)
        if dx == 0:
            return pltpu.make_async_remote_copy(
                jsend.at[column, turn(line, dy, lines)], jrecv.at[line, column], *sems,
                device_id=across(dy, 0), device_id_type=MESH)
        came = turn(column, -dx, columns)
        return pltpu.make_async_remote_copy(
            mid.at[turn(line, dy, lines), came], jrecv.at[line, came], *sems,
            device_id=across(dy, 0), device_id_type=MESH)

    def junction_in(dy, dx):
        i = dy * columns + dx
        sems = junction_send.at[i], junction_recv.at[i]
        came = turn(column, -dx, columns)
        if dy == 0:
            return pltpu.make_async_remote_copy(
                jsend.at[0], mid.at[:, came], *sems, device_id=across(0, dx), device_id_type=MESH)
        return pltpu.make_async_remote_copy(
            jsend.at[0, 0], jrecv.at[turn(line, -dy, lines), came], *sems,
            device_id=across(dy, 0), device_id_type=MESH)

    steps = [(dy, dx) for dy in range(lines) for dx in range(columns) if dy + dx > 0]

    def pass_junctions():
        for dx in range(1, columns):
            junction_in(0, dx).wait_recv()
            for dy in range(1, lines):
                junction(dy, dx).start()

    def wall_swap(of):
        slot = pl.ds(of * per_slab, per_slab)
        return pltpu.make_async_remote_copy(
            walls.at[slot], walls.at[slot], wall_send.at[0], wall_recv.at[0],
            device_id={"slab": partner}, device_id_type=MESH)

    def wall(t, way, of):
        slot = pl.ds(of * (CORES * per_slab), CORES * per_slab)
        send, recv = (up_send, up_recv) if way > 0 else (down_send, down_recv)
        return pltpu.make_async_remote_copy(
            walls.at[slot], walls.at[slot], send.at[t], recv.at[t],
            device_id={"slab": slab + way * CORES}, device_id_type=MESH)

    def wall_sends(t):
        return [(above & (level >= t), wall(t, 1, level - t)), (below & (level + t < levels), wall(t, -1, level + t))]

    def wall_arrivals(t):
        return [(level > t, wall(t, 1, level - 1 - t)), (level + 1 + t < levels, wall(t, -1, level + 1 + t))]

    def pass_walls(t):
        if t == 0:
            wall_swap(partner).wait_recv()
        else:
            for there, copy in wall_arrivals(t - 1):
                pl.when(there)(copy.wait_recv)
        if t < levels - 1:
            for there, copy in wall_sends(t):
                pl.when(there)(copy.start)

    @pl.when(slab < slabs - 1)
    def _():
        halo_up().start()

    @pl.when(slab > 0)
    def _():
        halo_down().start()

    for dx in range(1, columns):
        junction(0, dx).start()
    for dy in range(1, lines):
        junction(dy, 0).start()
    wall_swap(slab).start()

    chosen = spread()
    quad_row[...] = jnp.zeros_like(quad_row)
    coarse_row[...] = jnp.zeros_like(coarse_row)
    quad_row[:, 0:fine_points] = quad[...][None]
    coarse_row[:, 0:points] = coarse[...][None]
    tail[...] = jnp.zeros_like(tail)
    rows[...] = jnp.zeros_like(rows)
    xs[...] = jnp.zeros_like(xs)
    norms = split(coords[0] * coords[0] + coords[1] * coords[1] + coords[2] * coords[2], 3)
    rows[6:9] = jnp.ones((3, pt), F32)
    for c in range(count):
        for i in range(3):
            xs[c, i:i + 1, 0:points] = coords[i][c:c + 1]
            rows[i:i + 1, 0:points] = coords[i][c:c + 1]
            rows[3 + i:4 + i, 0:points] = norms[i][c:c + 1]
        xt[c] = rows[...].T[0:rows_t].astype(BF16)

    def repeat(raw):
        return jnp.dot(chosen, raw, preferred_element_type=F32)

    def distance(target, near_rows):
        return jnp.dot(xt[target], near_rows, preferred_element_type=F32)

    def weigh(value):
        inverse = lax.rsqrt(value)
        return (inverse * inverse * inverse).astype(BF16)

    def reduce(weights, value):
        sums = lax.dot_general(weights, value, (((1,), (1,)), ((), ())), preferred_element_type=F32)
        return sums[0:TERMS] + sums[TERMS:2 * TERMS] + sums[2 * TERMS:3 * TERMS]

    totals = {}
    pass_walls(0)

    def run(units, between={}):
        held = []
        for k in range(0, len(units) + 2, 2):
            for act in between.get(k // 2, ()):
                act()
            fresh = []
            for item, target, make in units[k:k + 2]:
                near_rows, weights = features(*make())
                fresh.append((item, weights, distance(target, near_rows)))
            sums = [(item, reduce(weights, value)) for item, weights, value in held]
            held = [(item, weights, weigh(value)) for item, weights, value in fresh]
            for item, value in sums:
                totals[item] = totals[item] + value if item in totals else value

    @pl.when(slab > 0)
    def _():
        halo_up().wait_recv()

    @pl.when(slab < slabs - 1)
    def _():
        halo_down().wait_recv()

    big.wait()
    lhs = jnp.concatenate([repeat(cells[pair_source[0, k]]) for k in range(pairs)], axis=0)[:, 0:points].astype(BF16)

    def fine(start):
        stop = min(start + WIDE, fine_points)
        value = jnp.dot(lhs, ups[:, start:stop], preferred_element_type=F32)
        if stop - start < WIDE:
            tail[:, 0:stop - start] = value
            value = tail[:, 0:up(stop - start, LANES)]
        return value.astype(BF16).astype(F32)

    units = []
    for start in range(0, fine_points, WIDE):
        cache = []

        def make(k, start=start, cache=cache):
            if not cache:
                cache.append(fine(start))
            value = cache[0][3 * TERMS * k:3 * TERMS * (k + 1)]
            return value, quad_row[:, start:start + value.shape[1]]

        units += [(("pair", k), pair_target[0, k], functools.partial(make, k)) for k in range(pairs)]
    between = {RELAY: [pass_junctions]}
    for t in range(1, levels - 1):
        between.setdefault(RELAY + RELAY_STEP * (t - 1), []).append(functools.partial(pass_walls, t))
    end = len(units) // 2
    run(units, {k: acts for k, acts in between.items() if k <= end})

    for dy, dx in steps:
        if dy > 0:
            junction_in(dy, dx).wait_recv()
    units = []
    for start in range(0, pt, WIDE):
        for dy, dx in steps:
            def make(start=start, dy=dy, dx=dx):
                at = slice(start, min(start + WIDE, pt))
                source = (mid if dy == 0 else jrecv)[turn(line, -dy, lines), turn(column, -dx, columns), :, at]
                return repeat(source), coarse_row[:, at]

            units.append((("junction", dy, dx), junction_target[0, 0, across(-dy, -dx)["seg"]], make))
    run(units)

    for k in sorted(between):
        if k > end:
            for act in between[k]:
                act()
    pass_walls(levels - 1)
    units = []
    for c in range(count):
        def make(c=c):
            value = repeat(jnp.concatenate([walls[wall_near[0, n, c]] for n in range(near)], axis=1))
            return value, WALL_GAIN

        units.append((("wall", c), c, make))
    run(units)

    places = [(("pair", k), pair_target[0, k]) for k in range(pairs)]
    places += [(("junction", dy, dx), junction_target[0, 0, across(-dy, -dx)["seg"]]) for dy, dx in steps]
    for c in range(count):
        total = totals["wall", c]
        for item, target in places:
            total = total + jnp.where(target == c, 1.0, 0.0) * totals[item]
        total = total[:, 0:points]
        x = xs[c, :, 0:points]
        x = [x[i:i + 1] for i in range(3)]
        a, b, h = total[0:3], [total[3 + 3 * i:6 + 3 * i] for i in range(3)], total[12:15]
        square = x[0] * x[0] + x[1] * x[1] + x[2] * x[2] + 2.0 * EPSILON2
        value = square * a + h - 2.0 * (x[0] * b[0] + x[1] * b[1] + x[2] * b[2])
        trace = b[0][0:1] + b[1][1:2] + b[2][2:3]
        lift = x[0] * a[0:1] + x[1] * a[1:2] + x[2] * a[2:3] - trace
        for i in range(3):
            along = x[0] * b[i][0:1] + x[1] * b[i][1:2] + x[2] * b[i][2:3]
            out[0, i, c:c + 1] = (value[i:i + 1] + x[i] * lift - along) * (1.0 / (8.0 * math.pi))

    @pl.when(slab < slabs - 1)
    def _():
        halo_up().wait_send()

    @pl.when(slab > 0)
    def _():
        halo_down().wait_send()

    for dy, dx in steps:
        junction(dy, dx).wait_send()
    wall_swap(slab).wait_send()
    for t in range(levels - 1):
        for there, copy in wall_sends(t):
            pl.when(there)(copy.wait_send)


def local(segs, slabs, positions, density, upsample, quad_weights, coarse_weights, pair_target, pair_source,
          junction_cell, junction_target, wall_points, wall_traction, wall_near):
    count, points = positions.shape[1], positions.shape[3]
    turned = (1, 3, count, points)
    fine_points = upsample.shape[1]
    pairs, near = pair_target.shape[1], wall_near.shape[2]
    per_slab, patch = wall_points.shape[1], wall_points.shape[3]
    cfg = (count, points, fine_points, pairs, near, patch, segs, slabs, per_slab)
    pt = up(points, LANES)
    lines, columns = grid(segs)
    levels = slabs // CORES
    vmem = pl.BlockSpec(memory_space=pltpu.VMEM)
    far = pl.BlockSpec(memory_space=pl.ANY)
    dma = pltpu.SemaphoreType.DMA
    result = pl.pallas_call(
        functools.partial(kernel, cfg),
        out_shape=pltpu.VMEM(turned, F32),
        in_specs=[far] * 12,
        out_specs=vmem,
        scratch_shapes=[
            pltpu.SMEM(pair_target.shape, jnp.int32),
            pltpu.SMEM(pair_source.shape, jnp.int32),
            pltpu.SMEM(junction_cell.shape, jnp.int32),
            pltpu.SMEM(junction_target.shape, jnp.int32),
            pltpu.SMEM((1, near, count), jnp.int32),
            pltpu.VMEM(quad_weights.shape, F32),
            pltpu.VMEM(coarse_weights.shape, F32),
            pltpu.VMEM((2,) + turned[1:], BF16),
            pltpu.VMEM((count, RAW, pt), BF16),
            pltpu.VMEM((count + 2 * HALO, RAW, pt), BF16),
            pltpu.VMEM((columns, lines, RAW, pt), BF16),
            pltpu.VMEM((lines, columns, RAW, pt), BF16),
            pltpu.VMEM((lines, columns, RAW, pt), BF16),
            pltpu.VMEM((2, per_slab, 3, patch), BF16),
            pltpu.VMEM((slabs * per_slab, RAW, patch), BF16),
            pltpu.VMEM(upsample.shape, BF16),
            pltpu.VMEM((TERMS, pt), F32),
            pltpu.VMEM((1, up(fine_points, LANES)), F32),
            pltpu.VMEM((1, pt), F32),
            pltpu.VMEM((3 * TERMS * pairs, WIDE), F32),
            pltpu.VMEM((count, up(points, 16), TERMS), BF16),
            pltpu.VMEM((count, 3, pt), F32),
            dma((12,)), dma((2,)), dma((2,)), dma((segs,)), dma((segs,)), dma((1,)), dma((1,)),
            dma((levels,)), dma((levels,)), dma((levels,)), dma((levels,)),
        ],
        compiler_params=pltpu.CompilerParams(collective_id=0, has_side_effects=True),
    )(pair_target, pair_source, junction_cell, junction_target, wall_near.transpose(0, 2, 1),
      positions.transpose(0, 2, 1, 3), density.transpose(0, 2, 1, 3), upsample, quad_weights, coarse_weights,
      wall_points, wall_traction)
    return result.transpose(0, 2, 1, 3)


def solution(mesh):
    placed = (
        P("seg", "slab", None, None),
        P("seg", "slab", None, None),
        P(),
        P(),
        P(),
        P("seg", "slab"),
        P("seg", "slab"),
        P("seg", "slab", None),
        P("seg", "slab", None),
        P("seg", "slab", None, None),
        P("seg", "slab", None, None),
        P("seg", "slab", None),
    )
    body = functools.partial(local, mesh.shape["seg"], mesh.shape["slab"])
    return jax.shard_map(
        body, mesh=mesh, in_specs=placed, out_specs=P("seg", "slab", None, None), check_vma=False
    )
```

```python
import functools
import math

import jax
import jax.numpy as jnp
from jax import lax
from jax.experimental import pallas as pl
from jax.experimental.pallas import tpu as pltpu
from jax.sharding import PartitionSpec as P

MESH = pl.DeviceIdType.MESH
HALO = 2
EPSILON2 = 0.05
WALL_GAIN = 3.0
LANES = 128
WIDE = 2 * LANES
TERMS = 16
SPLITS = 3
RAW = 6
PART = 3 * WIDE
CORES = 2
RELAY = 3
RELAY_STEP = 4
F32 = jnp.float32
BF16 = jnp.bfloat16


def up(n, m):
    return -(-n // m) * m


def grid(n):
    columns = max(k for k in range(1, n + 1) if n % k == 0 and k * k <= n)
    return n // columns, columns


def split(value, parts):
    out = []
    for _ in range(parts):
        piece = value.astype(BF16).astype(F32)
        out.append(piece)
        value = value - piece
    return out


def spread():
    shape = (3 * TERMS, RAW)
    r, c = (lax.broadcasted_iota(jnp.int32, shape, d) for d in range(2))

    def steps(first, count):
        return sum(jnp.where(r >= first + 3 * (k + 1), 1, 0) for k in range(count))

    at = jnp.where(
        r < 15, 3 + r - 3 * steps(0, 4), jnp.where(
            (r >= 19) & (r < 28), steps(19, 2), jnp.where(
                (r >= 28) & (r < 31), r - 28, jnp.where(
                    (r >= 32) & (r < 35), r - 32, jnp.where((r >= 40) & (r < 43), r - 37, -1)))))
    return jnp.where(c == at, jnp.where((r >= 32) & (r < 35), -2.0, 1.0), 0.0).astype(BF16)


def features(rep, weight):
    lanes = rep.shape[1]
    row = lax.broadcasted_iota(jnp.int32, (8, lanes), 0)
    y2, g = rep[32:40], rep[40:48]
    norm = 0.25 * jnp.sum(y2 * y2, axis=0, keepdims=True)
    dot = -0.5 * weight * jnp.sum(y2 * g, axis=0, keepdims=True)
    m = split(norm + EPSILON2, 3)
    first = jnp.where((row >= 3) & (row < 6), 1.0, y2)
    first = jnp.where(row == 6, m[0], jnp.where(row == 7, m[1], first))
    second = jnp.where(row == 0, m[2], 0.0)
    near = jnp.concatenate([first, second], axis=0).astype(BF16)
    one = rep[0:8] * weight * jnp.where(row < 3, 1.0, rep[16:24])
    two = rep[8:16] * weight * jnp.where(row >= 4, norm, rep[24:32])
    two = two + jnp.where(row >= 4, dot * rep[24:32], 0.0)
    parts = split(jnp.concatenate([one, two], axis=0), SPLITS)
    return near, jnp.concatenate(parts, axis=0).astype(BF16)


def kernel(
    cfg,
    pair_target_far, pair_source_far, junction_cell_far, junction_target_far, wall_near_far,
    positions, density, upsample, quad_far, coarse_far, wall_points, wall_traction,
    out,
    pair_target, pair_source, junction_cell, junction_target, wall_near, quad, coarse,
    own, mine, jsend, mid, jrecv, wall_own, walls, ups, rows, quad_row, coarse_row, xt, xs, held,
    local_sem, halo_send, halo_recv, junction_send, junction_recv, wall_send, wall_recv, up_send, up_recv, down_send, down_recv, *fine,
):
    count, points, fine_points, pairs, near, patch, segs, slabs, per_slab = cfg
    pt = xs.shape[2]
    rows_t = xt.shape[1]
    seg, slab = lax.axis_index("seg"), lax.axis_index("slab")
    lines, columns = grid(segs)
    levels = slabs // CORES
    line, column = lax.div(seg, columns), lax.rem(seg, columns)
    level, core = lax.div(slab, CORES), lax.rem(slab, CORES)
    partner = slab + 1 - 2 * core
    above, below = level < levels - 1, level > 0

    def turn(base, o, size):
        return lax.rem(base + (o + size), size)

    def across(dy, dx):
        return {"seg": turn(line, dy, lines) * columns + turn(column, dx, columns)}

    barrier = pltpu.get_barrier_semaphore()

    def greet(device):
        pl.semaphore_signal(barrier, inc=1, device_id=device, device_id_type=MESH)

    @pl.when(above)
    def _():
        greet({"slab": slab + CORES})

    @pl.when(below)
    def _():
        greet({"slab": slab - CORES})

    @pl.when((core == 1) & above)
    def _():
        greet({"slab": slab + 1})

    @pl.when((core == 0) & below)
    def _():
        greet({"slab": slab - 1})

    for dx in range(1, columns):
        greet(across(0, dx))
    for dy in range(1, lines):
        greet(across(dy, 0))
    greet({"slab": partner})

    copies = [
        pltpu.make_async_copy(positions.at[0], own.at[0], local_sem.at[0]),
        pltpu.make_async_copy(density.at[0], own.at[1], local_sem.at[1]),
        pltpu.make_async_copy(wall_points.at[0], wall_own.at[0], local_sem.at[2]),
        pltpu.make_async_copy(wall_traction.at[0], wall_own.at[1], local_sem.at[3]),
    ]
    big = pltpu.make_async_copy(upsample, ups, local_sem.at[4])
    tables = [
        pltpu.make_async_copy(source, target, local_sem.at[5 + i]) for i, (source, target) in enumerate([
            (pair_target_far, pair_target), (pair_source_far, pair_source), (junction_cell_far, junction_cell),
            (junction_target_far, junction_target), (wall_near_far, wall_near), (quad_far, quad), (coarse_far, coarse)])
    ]
    for copy in copies + tables:
        copy.start()
    big.start()
    for copy in copies + tables:
        copy.wait()

    mine[...] = jnp.zeros_like(mine)

    parts = [(start, part.shape[2]) for start, part in zip(range(0, up(fine_points, LANES), PART), fine)]
    for part in fine:
        @pl.when(slab == 0)
        def _():
            part[0:HALO] = jnp.zeros((HALO,) + part.shape[1:], BF16)

        @pl.when(slab == slabs - 1)
        def _():
            part[HALO + count:] = jnp.zeros((HALO,) + part.shape[1:], BF16)

    coords = [own[0, i].astype(F32) for i in range(3)]
    loads = [own[1, i].astype(F32) for i in range(3)]
    rest = jnp.zeros((8 - RAW, points), F32)
    raws = [jnp.concatenate([line[c:c + 1] for line in coords + loads] + [rest], axis=0) for c in range(count)]
    for c in range(count):
        mine[c, :, 0:points] = raws[c][0:RAW].astype(BF16)
    lhs = jnp.concatenate(raws, axis=0).astype(BF16)
    for b in range(segs):
        jsend[b % columns, b // columns] = mine[junction_cell[0, 0, b]]
    for p in range(per_slab):
        walls[slab * per_slab + p] = jnp.concatenate(
            [wall_own[0, p].astype(F32), wall_own[1, p].astype(F32)], axis=0).astype(BF16)
    chosen = spread()
    quad_row[...] = jnp.zeros_like(quad_row)
    coarse_row[...] = jnp.zeros_like(coarse_row)
    quad_row[:, 0:fine_points] = quad[...][None]
    coarse_row[:, 0:points] = coarse[...][None]
    rows[...] = jnp.zeros_like(rows)
    xs[...] = jnp.zeros_like(xs)
    norms = split(coords[0] * coords[0] + coords[1] * coords[1] + coords[2] * coords[2], 3)
    rows[6:9] = jnp.ones((3, pt), F32)
    for c in range(count):
        for i in range(3):
            xs[c, i:i + 1, 0:points] = coords[i][c:c + 1]
            rows[i:i + 1, 0:points] = coords[i][c:c + 1]
            rows[3 + i:4 + i, 0:points] = norms[i][c:c + 1]
        xt[c] = rows[...].T[0:rows_t].astype(BF16)

    big.wait()
    for (start, size), part in zip(parts, fine):
        for at in range(0, size, WIDE):
            stop = min(start + at + WIDE, fine_points)
            value = jnp.dot(lhs, ups[:, start + at:stop], preferred_element_type=F32)
            width = min(WIDE, size - at)
            if stop - start - at < width:
                value = jnp.concatenate([value, jnp.zeros((8 * count, width - value.shape[1]), F32)], axis=1)
            for c in range(count):
                part[HALO + c, :, at:at + width] = value[8 * c:8 * c + RAW].astype(BF16)
    beside = jnp.where(above, 1, 0) + jnp.where(below, 1, 0) + jnp.where(core == 1, jnp.where(above, 1, 0), jnp.where(below, 1, 0))
    pl.semaphore_wait(barrier, lines - 1 + columns - 1 + 1 + beside)

    def halo_up(p):
        return pltpu.make_async_remote_copy(
            fine[p].at[pl.ds(count, HALO)], fine[p].at[pl.ds(0, HALO)], halo_send.at[0, p], halo_recv.at[0, p],
            device_id={"slab": lax.rem(slab + 1, slabs)}, device_id_type=MESH)

    def halo_down(p):
        return pltpu.make_async_remote_copy(
            fine[p].at[pl.ds(HALO, HALO)], fine[p].at[pl.ds(HALO + count, HALO)], halo_send.at[1, p], halo_recv.at[1, p],
            device_id={"slab": lax.rem(slab + slabs - 1, slabs)}, device_id_type=MESH)

    def junction(dy, dx):
        i = dy * columns + dx
        sems = junction_send.at[i], junction_recv.at[i]
        if dy == 0:
            return pltpu.make_async_remote_copy(
                jsend.at[turn(column, dx, columns)], mid.at[:, column], *sems,
                device_id=across(0, dx), device_id_type=MESH)
        if dx == 0:
            return pltpu.make_async_remote_copy(
                jsend.at[column, turn(line, dy, lines)], jrecv.at[line, column], *sems,
                device_id=across(dy, 0), device_id_type=MESH)
        came = turn(column, -dx, columns)
        return pltpu.make_async_remote_copy(
            mid.at[turn(line, dy, lines), came], jrecv.at[line, came], *sems,
            device_id=across(dy, 0), device_id_type=MESH)

    def junction_in(dy, dx):
        i = dy * columns + dx
        sems = junction_send.at[i], junction_recv.at[i]
        came = turn(column, -dx, columns)
        if dy == 0:
            return pltpu.make_async_remote_copy(
                jsend.at[0], mid.at[:, came], *sems, device_id=across(0, dx), device_id_type=MESH)
        return pltpu.make_async_remote_copy(
            jsend.at[0, 0], jrecv.at[turn(line, -dy, lines), came], *sems,
            device_id=across(dy, 0), device_id_type=MESH)

    steps = [(dy, dx) for dy in range(lines) for dx in range(columns) if dy + dx > 0]

    def pass_junctions():
        for dx in range(1, columns):
            junction_in(0, dx).wait_recv()
            for dy in range(1, lines):
                junction(dy, dx).start()

    def wall_swap(of):
        slot = pl.ds(of * per_slab, per_slab)
        return pltpu.make_async_remote_copy(
            walls.at[slot], walls.at[slot], wall_send.at[0], wall_recv.at[0],
            device_id={"slab": partner}, device_id_type=MESH)

    def wall(t, way, of):
        slot = pl.ds(of * (CORES * per_slab), CORES * per_slab)
        send, recv = (up_send, up_recv) if way > 0 else (down_send, down_recv)
        return pltpu.make_async_remote_copy(
            walls.at[slot], walls.at[slot], send.at[t], recv.at[t],
            device_id={"slab": slab + way * CORES}, device_id_type=MESH)

    def wall_sends(t):
        return [(above & (level >= t), wall(t, 1, level - t)), (below & (level + t < levels), wall(t, -1, level + t))]

    def wall_arrivals(t):
        return [(level > t, wall(t, 1, level - 1 - t)), (level + 1 + t < levels, wall(t, -1, level + 1 + t))]

    def pass_walls(t):
        if t == 0:
            wall_swap(partner).wait_recv()
        else:
            for there, copy in wall_arrivals(t - 1):
                pl.when(there)(copy.wait_recv)
        if t < levels - 1:
            for there, copy in wall_sends(t):
                pl.when(there)(copy.start)

    for p in range(len(fine)):
        pl.when(slab < slabs - 1)(halo_up(p).start)
        pl.when(slab > 0)(halo_down(p).start)
    for dx in range(1, columns):
        junction(0, dx).start()
    for dy in range(1, lines):
        junction(dy, 0).start()
    wall_swap(slab).start()

    def repeat(raw):
        return jnp.dot(chosen, raw, preferred_element_type=F32)

    def distance(target, near_rows):
        return jnp.dot(xt[target], near_rows, preferred_element_type=F32)

    def weigh(value):
        inverse = lax.rsqrt(value)
        return (inverse * inverse * inverse).astype(BF16)

    def reduce(weights, value):
        sums = lax.dot_general(weights, value, (((1,), (1,)), ((), ())), preferred_element_type=F32)
        return sums[0:TERMS] + sums[TERMS:2 * TERMS] + sums[2 * TERMS:3 * TERMS]

    totals = {}
    pass_walls(0)

    def run(units, between={}):
        before = []
        for k in range(0, len(units) + 2, 2):
            for act in between.get(k // 2, ()):
                act()
            fresh = []
            for u, (item, target, make) in enumerate(units[k:k + 2]):
                near_rows, weights = features(*make())
                at = held.at[k // 2 % 2, u, :, 0:near_rows.shape[1]]
                at[...] = weigh(distance(target, near_rows))
                fresh.append((item, weights, at))
            for item, weights, at in before:
                value = reduce(weights, at[...])
                totals[item] = totals[item] + value if item in totals else value
            before = fresh

    def arrive(p):
        pl.when(slab > 0)(halo_up(p).wait_recv)
        pl.when(slab < slabs - 1)(halo_down(p).wait_recv)

    between = {}
    units = []
    for p, (start, size) in enumerate(parts):
        between[len(units) // pairs * pairs // 2] = [functools.partial(arrive, p)]
        for at in range(0, size, WIDE):
            for k in range(pairs):
                def make(k=k, p=p, at=at, start=start, stop=min(at + WIDE, size)):
                    return repeat(fine[p][pair_source[0, k], :, at:stop]), quad_row[:, start + at:start + stop]

                units.append((("pair", k), pair_target[0, k], make))
    between.setdefault(RELAY, []).append(pass_junctions)
    for t in range(1, levels - 1):
        between.setdefault(RELAY + RELAY_STEP * (t - 1), []).append(functools.partial(pass_walls, t))
    end = len(units) // 2
    run(units, {k: acts for k, acts in between.items() if k <= end})

    for dy, dx in steps:
        if dy > 0:
            junction_in(dy, dx).wait_recv()
    units = []
    for start in range(0, pt, WIDE):
        for dy, dx in steps:
            def make(start=start, dy=dy, dx=dx):
                at = slice(start, min(start + WIDE, pt))
                source = (mid if dy == 0 else jrecv)[turn(line, -dy, lines), turn(column, -dx, columns), :, at]
                return repeat(source), coarse_row[:, at]

            units.append((("junction", dy, dx), junction_target[0, 0, across(-dy, -dx)["seg"]], make))
    run(units)

    for k in sorted(between):
        if k > end:
            for act in between[k]:
                act()
    pass_walls(levels - 1)
    units = []
    for c in range(count):
        def make(c=c):
            value = repeat(jnp.concatenate([walls[wall_near[0, n, c]] for n in range(near)], axis=1))
            return value, WALL_GAIN

        units.append((("wall", c), c, make))
    run(units)

    places = [(("pair", k), pair_target[0, k]) for k in range(pairs)]
    places += [(("junction", dy, dx), junction_target[0, 0, across(-dy, -dx)["seg"]]) for dy, dx in steps]
    for c in range(count):
        total = totals["wall", c]
        for item, target in places:
            total = total + jnp.where(target == c, 1.0, 0.0) * totals[item]
        total = total[:, 0:points]
        x = xs[c, :, 0:points]
        x = [x[i:i + 1] for i in range(3)]
        a, b, h = total[0:3], [total[3 + 3 * i:6 + 3 * i] for i in range(3)], total[12:15]
        square = x[0] * x[0] + x[1] * x[1] + x[2] * x[2] + 2.0 * EPSILON2
        value = square * a + h - 2.0 * (x[0] * b[0] + x[1] * b[1] + x[2] * b[2])
        trace = b[0][0:1] + b[1][1:2] + b[2][2:3]
        lift = x[0] * a[0:1] + x[1] * a[1:2] + x[2] * a[2:3] - trace
        for i in range(3):
            along = x[0] * b[i][0:1] + x[1] * b[i][1:2] + x[2] * b[i][2:3]
            out[0, i, c:c + 1] = (value[i:i + 1] + x[i] * lift - along) * (1.0 / (8.0 * math.pi))

    for p in range(len(fine)):
        pl.when(slab < slabs - 1)(halo_up(p).wait_send)
        pl.when(slab > 0)(halo_down(p).wait_send)
    for dy, dx in steps:
        junction(dy, dx).wait_send()
    wall_swap(slab).wait_send()
    for t in range(levels - 1):
        for there, copy in wall_sends(t):
            pl.when(there)(copy.wait_send)


def local(segs, slabs, positions, density, upsample, quad_weights, coarse_weights, pair_target, pair_source,
          junction_cell, junction_target, wall_points, wall_traction, wall_near):
    count, points = positions.shape[1], positions.shape[3]
    turned = (1, 3, count, points)
    fine_points = upsample.shape[1]
    pairs, near = pair_target.shape[1], wall_near.shape[2]
    per_slab, patch = wall_points.shape[1], wall_points.shape[3]
    cfg = (count, points, fine_points, pairs, near, patch, segs, slabs, per_slab)
    pt = up(points, LANES)
    lines, columns = grid(segs)
    levels = slabs // CORES
    widths = [min(PART, up(fine_points, LANES) - start) for start in range(0, up(fine_points, LANES), PART)]
    vmem = pl.BlockSpec(memory_space=pltpu.VMEM)
    far = pl.BlockSpec(memory_space=pl.ANY)
    dma = pltpu.SemaphoreType.DMA
    result = pl.pallas_call(
        functools.partial(kernel, cfg),
        out_shape=pltpu.VMEM(turned, F32),
        in_specs=[far] * 12,
        out_specs=vmem,
        scratch_shapes=[
            pltpu.SMEM(pair_target.shape, jnp.int32),
            pltpu.SMEM(pair_source.shape, jnp.int32),
            pltpu.SMEM(junction_cell.shape, jnp.int32),
            pltpu.SMEM(junction_target.shape, jnp.int32),
            pltpu.SMEM((1, near, count), jnp.int32),
            pltpu.VMEM(quad_weights.shape, F32),
            pltpu.VMEM(coarse_weights.shape, F32),
            pltpu.VMEM((2,) + turned[1:], BF16),
            pltpu.VMEM((count, RAW, pt), BF16),
            pltpu.VMEM((columns, lines, RAW, pt), BF16),
            pltpu.VMEM((lines, columns, RAW, pt), BF16),
            pltpu.VMEM((lines, columns, RAW, pt), BF16),
            pltpu.VMEM((2, per_slab, 3, patch), BF16),
            pltpu.VMEM((slabs * per_slab, RAW, patch), BF16),
            pltpu.VMEM(upsample.shape, BF16),
            pltpu.VMEM((TERMS, pt), F32),
            pltpu.VMEM((1, up(fine_points, LANES)), F32),
            pltpu.VMEM((1, pt), F32),
            pltpu.VMEM((count, up(points, 16), TERMS), BF16),
            pltpu.VMEM((count, 3, pt), F32),
            pltpu.VMEM((2, 2, up(points, 16), WIDE), BF16),
            dma((12,)), dma((2, len(widths))), dma((2, len(widths))), dma((segs,)), dma((segs,)), dma((1,)), dma((1,)),
            dma((levels,)), dma((levels,)), dma((levels,)), dma((levels,)),
            *[pltpu.VMEM((count + 2 * HALO, RAW, width), BF16) for width in widths],
        ],
        compiler_params=pltpu.CompilerParams(collective_id=0, has_side_effects=True),
    )(pair_target, pair_source, junction_cell, junction_target, wall_near.transpose(0, 2, 1),
      positions.transpose(0, 2, 1, 3), density.transpose(0, 2, 1, 3), upsample, quad_weights, coarse_weights,
      wall_points, wall_traction)
    return result.transpose(0, 2, 1, 3)


def solution(mesh):
    placed = (
        P("seg", "slab", None, None),
        P("seg", "slab", None, None),
        P(),
        P(),
        P(),
        P("seg", "slab"),
        P("seg", "slab"),
        P("seg", "slab", None),
        P("seg", "slab", None),
        P("seg", "slab", None, None),
        P("seg", "slab", None, None),
        P("seg", "slab", None),
    )
    body = functools.partial(local, mesh.shape["seg"], mesh.shape["slab"])
    return jax.shard_map(
        body, mesh=mesh, in_specs=placed, out_specs=P("seg", "slab", None, None), check_vma=False
    )
```

```python
import functools
import math

import jax
import jax.numpy as jnp
from jax import lax
from jax.experimental import pallas as pl
from jax.experimental.pallas import tpu as pltpu
from jax.sharding import PartitionSpec as P

MESH = pl.DeviceIdType.MESH
HALO = 2
EPSILON2 = 0.05
WALL_GAIN = 3.0
LANES = 128
WIDE = 2 * LANES
TERMS = 16
SPLITS = 3
RAW = 6
PARTS = (2 * WIDE, 4 * WIDE)
CORES = 2
RELAY = 3
RELAY_STEP = 4
F32 = jnp.float32
BF16 = jnp.bfloat16


def up(n, m):
    return -(-n // m) * m


def cuts(n):
    out, start, stop = [], 0, up(n, LANES)
    for width in PARTS + (stop,):
        if start < stop:
            out.append((start, min(width, stop - start)))
            start += out[-1][1]
    return out


def grid(n):
    columns = max(k for k in range(1, n + 1) if n % k == 0 and k * k <= n)
    return n // columns, columns


def split(value, parts):
    out = []
    for _ in range(parts):
        piece = value.astype(BF16).astype(F32)
        out.append(piece)
        value = value - piece
    return out


def spread():
    shape = (3 * TERMS, RAW)
    r, c = (lax.broadcasted_iota(jnp.int32, shape, d) for d in range(2))

    def steps(first, count):
        return sum(jnp.where(r >= first + 3 * (k + 1), 1, 0) for k in range(count))

    at = jnp.where(
        r < 15, 3 + r - 3 * steps(0, 4), jnp.where(
            (r >= 19) & (r < 28), steps(19, 2), jnp.where(
                (r >= 28) & (r < 31), r - 28, jnp.where(
                    (r >= 32) & (r < 35), r - 32, jnp.where((r >= 40) & (r < 43), r - 37, -1)))))
    return jnp.where(c == at, jnp.where((r >= 32) & (r < 35), -2.0, 1.0), 0.0).astype(BF16)


def features(rep, weight):
    lanes = rep.shape[1]
    row = lax.broadcasted_iota(jnp.int32, (8, lanes), 0)
    y2, g = rep[32:40], rep[40:48]
    norm = 0.25 * jnp.sum(y2 * y2, axis=0, keepdims=True)
    dot = -0.5 * weight * jnp.sum(y2 * g, axis=0, keepdims=True)
    m = split(norm + EPSILON2, 3)
    first = jnp.where((row >= 3) & (row < 6), 1.0, y2)
    first = jnp.where(row == 6, m[0], jnp.where(row == 7, m[1], first))
    second = jnp.where(row == 0, m[2], 0.0)
    near = jnp.concatenate([first, second], axis=0).astype(BF16)
    one = rep[0:8] * weight * jnp.where(row < 3, 1.0, rep[16:24])
    two = rep[8:16] * weight * jnp.where(row >= 4, norm, rep[24:32])
    two = two + jnp.where(row >= 4, dot * rep[24:32], 0.0)
    parts = split(jnp.concatenate([one, two], axis=0), SPLITS)
    return near, jnp.concatenate(parts, axis=0).astype(BF16)


def kernel(
    cfg,
    pair_target_far, pair_source_far, junction_cell_far, junction_target_far, wall_near_far,
    positions, density, upsample, quad_far, coarse_far, wall_points, wall_traction,
    out,
    pair_target, pair_source, junction_cell, junction_target, wall_near, quad, coarse,
    own, mine, jsend, mid, jrecv, wall_own, walls, ups, rows, quad_row, coarse_row, xt, xs, held, nears, weights,
    local_sem, halo_send, halo_recv, junction_send, junction_recv, wall_send, wall_recv, up_send, up_recv, down_send, down_recv, *fine,
):
    count, points, fine_points, pairs, near, patch, segs, slabs, per_slab = cfg
    pt, qp = xs.shape[2], quad_row.shape[1]
    rows_t = xt.shape[1]
    seg, slab = lax.axis_index("seg"), lax.axis_index("slab")
    lines, columns = grid(segs)
    levels = slabs // CORES
    line, column = lax.div(seg, columns), lax.rem(seg, columns)
    level, core = lax.div(slab, CORES), lax.rem(slab, CORES)
    partner = slab + 1 - 2 * core
    above, below = level < levels - 1, level > 0

    def turn(base, o, size):
        return lax.rem(base + (o + size), size)

    def across(dy, dx):
        return {"seg": turn(line, dy, lines) * columns + turn(column, dx, columns)}

    barrier = pltpu.get_barrier_semaphore()

    def greet(device):
        pl.semaphore_signal(barrier, inc=1, device_id=device, device_id_type=MESH)

    @pl.when(above)
    def _():
        greet({"slab": slab + CORES})

    @pl.when(below)
    def _():
        greet({"slab": slab - CORES})

    @pl.when((core == 1) & above)
    def _():
        greet({"slab": slab + 1})

    @pl.when((core == 0) & below)
    def _():
        greet({"slab": slab - 1})

    for dx in range(1, columns):
        greet(across(0, dx))
    for dy in range(1, lines):
        greet(across(dy, 0))
    greet({"slab": partner})

    copies = [
        pltpu.make_async_copy(positions.at[0], own.at[0], local_sem.at[0]),
        pltpu.make_async_copy(density.at[0], own.at[1], local_sem.at[1]),
        pltpu.make_async_copy(wall_points.at[0], wall_own.at[0], local_sem.at[2]),
        pltpu.make_async_copy(wall_traction.at[0], wall_own.at[1], local_sem.at[3]),
    ]
    big = pltpu.make_async_copy(upsample, ups, local_sem.at[4])
    tables = [
        pltpu.make_async_copy(source, target, local_sem.at[5 + i]) for i, (source, target) in enumerate([
            (pair_target_far, pair_target), (pair_source_far, pair_source), (junction_cell_far, junction_cell),
            (junction_target_far, junction_target), (wall_near_far, wall_near), (quad_far, quad), (coarse_far, coarse)])
    ]
    for copy in copies + tables:
        copy.start()
    big.start()
    for copy in copies + tables:
        copy.wait()

    mine[...] = jnp.zeros_like(mine)

    parts = cuts(fine_points)
    for part in fine:
        @pl.when(slab == 0)
        def _():
            part[0:HALO] = jnp.zeros((HALO,) + part.shape[1:], BF16)

        @pl.when(slab == slabs - 1)
        def _():
            part[HALO + count:] = jnp.zeros((HALO,) + part.shape[1:], BF16)

    coords = [own[0, i].astype(F32) for i in range(3)]
    loads = [own[1, i].astype(F32) for i in range(3)]
    rest = jnp.zeros((8 - RAW, points), F32)
    raws = [jnp.concatenate([line[c:c + 1] for line in coords + loads] + [rest], axis=0) for c in range(count)]
    for c in range(count):
        mine[c, :, 0:points] = raws[c][0:RAW].astype(BF16)
    lhs = jnp.concatenate(raws, axis=0).astype(BF16)
    for b in range(segs):
        jsend[b % columns, b // columns] = mine[junction_cell[0, 0, b]]
    for p in range(per_slab):
        walls[slab * per_slab + p] = jnp.concatenate(
            [wall_own[0, p].astype(F32), wall_own[1, p].astype(F32)], axis=0).astype(BF16)
    chosen = spread()
    quad_row[...] = jnp.zeros_like(quad_row)
    coarse_row[...] = jnp.zeros_like(coarse_row)
    quad_row[:, 0:fine_points] = quad[...][None]
    coarse_row[:, 0:points] = coarse[...][None]
    rows[...] = jnp.zeros_like(rows)
    xs[...] = jnp.zeros_like(xs)
    norms = split(coords[0] * coords[0] + coords[1] * coords[1] + coords[2] * coords[2], 3)
    rows[6:9] = jnp.ones((3, pt), F32)
    for c in range(count):
        for i in range(3):
            xs[c, i:i + 1, 0:points] = coords[i][c:c + 1]
            rows[i:i + 1, 0:points] = coords[i][c:c + 1]
            rows[3 + i:4 + i, 0:points] = norms[i][c:c + 1]
        xt[c] = rows[...].T[0:rows_t].astype(BF16)

    big.wait()
    for (start, size), part in zip(parts, fine):
        for at in range(0, size, WIDE):
            stop = min(start + at + WIDE, fine_points)
            value = jnp.dot(lhs, ups[:, start + at:stop], preferred_element_type=F32)
            width = min(WIDE, size - at)
            if stop - start - at < width:
                value = jnp.concatenate([value, jnp.zeros((8 * count, width - value.shape[1]), F32)], axis=1)
            for c in range(count):
                part[HALO + c, :, at:at + width] = value[8 * c:8 * c + RAW].astype(BF16)
    beside = jnp.where(above, 1, 0) + jnp.where(below, 1, 0) + jnp.where(core == 1, jnp.where(above, 1, 0), jnp.where(below, 1, 0))
    pl.semaphore_wait(barrier, lines - 1 + columns - 1 + 1 + beside)

    def halo_up(p):
        return pltpu.make_async_remote_copy(
            fine[p].at[pl.ds(count, HALO)], fine[p].at[pl.ds(0, HALO)], halo_send.at[0, p], halo_recv.at[0, p],
            device_id={"slab": lax.rem(slab + 1, slabs)}, device_id_type=MESH)

    def halo_down(p):
        return pltpu.make_async_remote_copy(
            fine[p].at[pl.ds(HALO, HALO)], fine[p].at[pl.ds(HALO + count, HALO)], halo_send.at[1, p], halo_recv.at[1, p],
            device_id={"slab": lax.rem(slab + slabs - 1, slabs)}, device_id_type=MESH)

    def junction(dy, dx):
        i = dy * columns + dx
        sems = junction_send.at[i], junction_recv.at[i]
        if dy == 0:
            return pltpu.make_async_remote_copy(
                jsend.at[turn(column, dx, columns)], mid.at[:, column], *sems,
                device_id=across(0, dx), device_id_type=MESH)
        if dx == 0:
            return pltpu.make_async_remote_copy(
                jsend.at[column, turn(line, dy, lines)], jrecv.at[line, column], *sems,
                device_id=across(dy, 0), device_id_type=MESH)
        came = turn(column, -dx, columns)
        return pltpu.make_async_remote_copy(
            mid.at[turn(line, dy, lines), came], jrecv.at[line, came], *sems,
            device_id=across(dy, 0), device_id_type=MESH)

    def junction_in(dy, dx):
        i = dy * columns + dx
        sems = junction_send.at[i], junction_recv.at[i]
        came = turn(column, -dx, columns)
        if dy == 0:
            return pltpu.make_async_remote_copy(
                jsend.at[0], mid.at[:, came], *sems, device_id=across(0, dx), device_id_type=MESH)
        return pltpu.make_async_remote_copy(
            jsend.at[0, 0], jrecv.at[turn(line, -dy, lines), came], *sems,
            device_id=across(dy, 0), device_id_type=MESH)

    steps = [(dy, dx) for dy in range(lines) for dx in range(columns) if dy + dx > 0]

    def pass_junctions():
        for dx in range(1, columns):
            junction_in(0, dx).wait_recv()
            for dy in range(1, lines):
                junction(dy, dx).start()

    def wall_swap(of):
        slot = pl.ds(of * per_slab, per_slab)
        return pltpu.make_async_remote_copy(
            walls.at[slot], walls.at[slot], wall_send.at[0], wall_recv.at[0],
            device_id={"slab": partner}, device_id_type=MESH)

    def wall(t, way, of):
        slot = pl.ds(of * (CORES * per_slab), CORES * per_slab)
        send, recv = (up_send, up_recv) if way > 0 else (down_send, down_recv)
        return pltpu.make_async_remote_copy(
            walls.at[slot], walls.at[slot], send.at[t], recv.at[t],
            device_id={"slab": slab + way * CORES}, device_id_type=MESH)

    def wall_sends(t):
        return [(above & (level >= t), wall(t, 1, level - t)), (below & (level + t < levels), wall(t, -1, level + t))]

    def wall_arrivals(t):
        return [(level > t, wall(t, 1, level - 1 - t)), (level + 1 + t < levels, wall(t, -1, level + 1 + t))]

    def pass_walls(t):
        if t == 0:
            wall_swap(partner).wait_recv()
        else:
            for there, copy in wall_arrivals(t - 1):
                pl.when(there)(copy.wait_recv)
        if t < levels - 1:
            for there, copy in wall_sends(t):
                pl.when(there)(copy.start)

    for p in range(len(fine)):
        pl.when(slab < slabs - 1)(halo_up(p).start)
        pl.when(slab > 0)(halo_down(p).start)
    for dx in range(1, columns):
        junction(0, dx).start()
    for dy in range(1, lines):
        junction(dy, 0).start()
    wall_swap(slab).start()

    def repeat(raw):
        return jnp.dot(chosen, raw, preferred_element_type=F32)

    def distance(target, near_rows):
        return jnp.dot(xt[target], near_rows, preferred_element_type=F32)

    def weigh(value):
        inverse = lax.rsqrt(value)
        return (inverse * inverse * inverse).astype(BF16)

    def reduce(weights, value):
        sums = lax.dot_general(weights, value, (((1,), (1,)), ((), ())), preferred_element_type=F32)
        return sums[0:TERMS] + sums[TERMS:2 * TERMS] + sums[2 * TERMS:3 * TERMS]

    totals = {}
    pass_walls(0)

    def run(units, between):
        before = []
        for k in range(0, len(units) + 2, 2):
            for act in between.get(k // 2, ()):
                act()
            fresh = []
            for u, (item, target, start, size) in enumerate(units[k:k + 2]):
                at = held.at[k // 2 % 2, u, :, 0:size]
                at[...] = weigh(distance(target, nears[:, start:start + size]))
                fresh.append((item, start, size, at))
            for item, start, size, at in before:
                value = reduce(weights[:, start:start + size], at[...])
                totals[item] = totals[item] + value if item in totals else value
            before = fresh

    def prepare(start, rep, weight):
        at = slice(start, start + rep.shape[1])
        nears[:, at], weights[:, at] = features(rep, weight)

    def arrive(p):
        pl.when(slab > 0)(halo_up(p).wait_recv)
        pl.when(slab < slabs - 1)(halo_down(p).wait_recv)

    def prepare_pairs(p):
        start, size = parts[p]
        for k in range(pairs):
            prepare(k * qp + start, repeat(fine[p][pair_source[0, k]]), quad_row[:, start:start + size])

    def prepare_junction(i, dy, dx):
        source = (mid if dy == 0 else jrecv)[turn(line, -dy, lines), turn(column, -dx, columns)]
        prepare(pairs * qp + i * pt, repeat(source), coarse_row[...])

    def prepare_walls():
        near_by = jnp.concatenate([walls[wall_near[0, n, c]] for c in range(count) for n in range(near)], axis=1)
        prepare(pairs * qp + len(steps) * pt, repeat(near_by), WALL_GAIN)

    steps = sorted(steps, key=lambda step: min(step) > 0)
    direct = [i for i, step in enumerate(steps) if min(step) == 0]
    relayed = [i for i, step in enumerate(steps) if min(step) > 0]

    def arrive_junctions(which):
        for i in which:
            if steps[i][0] > 0:
                junction_in(*steps[i]).wait_recv()
        for i in which:
            prepare_junction(i, *steps[i])

    units = []
    firsts = []
    for start, size in parts:
        firsts.append(len(units) // 2)
        for at in range(start, start + size, WIDE):
            units += [(("pair", k), pair_target[0, k], k * qp + at, min(WIDE, start + size - at)) for k in range(pairs)]

    def junction_units(which):
        return [
            (("junction",) + steps[i], junction_target[0, 0, across(-steps[i][0], -steps[i][1])["seg"]],
             pairs * qp + i * pt + at, min(WIDE, pt - at)) for at in range(0, pt, WIDE) for i in which]

    ends = [len(units) // 2]
    units += junction_units(direct)
    ends.append(len(units) // 2)
    units += junction_units(relayed)
    ends.append(len(units) // 2)
    base = pairs * qp + len(steps) * pt
    span = near * up(patch, LANES)
    for c in range(count):
        units += [(("wall", c), c, base + c * span + at, min(WIDE, span - at)) for at in range(0, span, WIDE)]

    between = {}

    def when(k, *acts):
        between.setdefault(k, []).extend(acts)

    last = len(parts) - 1
    when(0, *[functools.partial(f, 0) for f in (arrive, prepare_pairs)])
    for p in range(1, len(parts)):
        when(firsts[p - 1], functools.partial(arrive, p))
        if p == min(2, last):
            when(firsts[p - 1], pass_junctions)
        if 1 < p <= levels - 1:
            when(firsts[p - 1], functools.partial(pass_walls, p - 1))
        when(firsts[p - 1], functools.partial(prepare_pairs, p))
    done = max(last - 1, 0)
    if last == 0:
        when(0, pass_junctions)
    when(firsts[last], functools.partial(arrive_junctions, direct))
    if done + 1 < levels:
        when(firsts[last], functools.partial(pass_walls, done + 1))
    when(ends[0], functools.partial(arrive_junctions, relayed))
    when(ends[1], *[functools.partial(pass_walls, t) for t in range(done + 2, levels)], prepare_walls)
    run(units, between)

    places = [(("pair", k), pair_target[0, k]) for k in range(pairs)]
    places += [(("junction", dy, dx), junction_target[0, 0, across(-dy, -dx)["seg"]]) for dy, dx in steps]
    for c in range(count):
        total = totals["wall", c]
        for item, target in places:
            total = total + jnp.where(target == c, 1.0, 0.0) * totals[item]
        total = total[:, 0:points]
        x = xs[c, :, 0:points]
        x = [x[i:i + 1] for i in range(3)]
        a, b, h = total[0:3], [total[3 + 3 * i:6 + 3 * i] for i in range(3)], total[12:15]
        square = x[0] * x[0] + x[1] * x[1] + x[2] * x[2] + 2.0 * EPSILON2
        value = square * a + h - 2.0 * (x[0] * b[0] + x[1] * b[1] + x[2] * b[2])
        trace = b[0][0:1] + b[1][1:2] + b[2][2:3]
        lift = x[0] * a[0:1] + x[1] * a[1:2] + x[2] * a[2:3] - trace
        for i in range(3):
            along = x[0] * b[i][0:1] + x[1] * b[i][1:2] + x[2] * b[i][2:3]
            out[0, i, c:c + 1] = (value[i:i + 1] + x[i] * lift - along) * (1.0 / (8.0 * math.pi))

    for p in range(len(fine)):
        pl.when(slab < slabs - 1)(halo_up(p).wait_send)
        pl.when(slab > 0)(halo_down(p).wait_send)
    for dy, dx in steps:
        junction(dy, dx).wait_send()
    wall_swap(slab).wait_send()
    for t in range(levels - 1):
        for there, copy in wall_sends(t):
            pl.when(there)(copy.wait_send)


def local(segs, slabs, positions, density, upsample, quad_weights, coarse_weights, pair_target, pair_source,
          junction_cell, junction_target, wall_points, wall_traction, wall_near):
    count, points = positions.shape[1], positions.shape[3]
    turned = (1, 3, count, points)
    fine_points = upsample.shape[1]
    pairs, near = pair_target.shape[1], wall_near.shape[2]
    per_slab, patch = wall_points.shape[1], wall_points.shape[3]
    cfg = (count, points, fine_points, pairs, near, patch, segs, slabs, per_slab)
    pt = up(points, LANES)
    lines, columns = grid(segs)
    levels = slabs // CORES
    widths = [width for _, width in cuts(fine_points)]
    lanes = pairs * up(fine_points, LANES) + (segs - 1) * pt + count * near * up(patch, LANES)
    vmem = pl.BlockSpec(memory_space=pltpu.VMEM)
    far = pl.BlockSpec(memory_space=pl.ANY)
    dma = pltpu.SemaphoreType.DMA
    result = pl.pallas_call(
        functools.partial(kernel, cfg),
        out_shape=pltpu.VMEM(turned, F32),
        in_specs=[far] * 12,
        out_specs=vmem,
        scratch_shapes=[
            pltpu.SMEM(pair_target.shape, jnp.int32),
            pltpu.SMEM(pair_source.shape, jnp.int32),
            pltpu.SMEM(junction_cell.shape, jnp.int32),
            pltpu.SMEM(junction_target.shape, jnp.int32),
            pltpu.SMEM((1, near, count), jnp.int32),
            pltpu.VMEM(quad_weights.shape, F32),
            pltpu.VMEM(coarse_weights.shape, F32),
            pltpu.VMEM((2,) + turned[1:], BF16),
            pltpu.VMEM((count, RAW, pt), BF16),
            pltpu.VMEM((columns, lines, RAW, pt), BF16),
            pltpu.VMEM((lines, columns, RAW, pt), BF16),
            pltpu.VMEM((lines, columns, RAW, pt), BF16),
            pltpu.VMEM((2, per_slab, 3, patch), BF16),
            pltpu.VMEM((slabs * per_slab, RAW, patch), BF16),
            pltpu.VMEM(upsample.shape, BF16),
            pltpu.VMEM((TERMS, pt), F32),
            pltpu.VMEM((1, up(fine_points, LANES)), F32),
            pltpu.VMEM((1, pt), F32),
            pltpu.VMEM((count, up(points, 16), TERMS), BF16),
            pltpu.VMEM((count, 3, pt), F32),
            pltpu.VMEM((2, 2, up(points, 16), WIDE), BF16),
            pltpu.VMEM((TERMS, lanes), BF16),
            pltpu.VMEM((SPLITS * TERMS, lanes), BF16),
            dma((12,)), dma((2, len(widths))), dma((2, len(widths))), dma((segs,)), dma((segs,)), dma((1,)), dma((1,)),
            dma((levels,)), dma((levels,)), dma((levels,)), dma((levels,)),
            *[pltpu.VMEM((count + 2 * HALO, RAW, width), BF16) for width in widths],
        ],
        compiler_params=pltpu.CompilerParams(collective_id=0, has_side_effects=True),
    )(pair_target, pair_source, junction_cell, junction_target, wall_near.transpose(0, 2, 1),
      positions.transpose(0, 2, 1, 3), density.transpose(0, 2, 1, 3), upsample, quad_weights, coarse_weights,
      wall_points, wall_traction)
    return result.transpose(0, 2, 1, 3)


def solution(mesh):
    placed = (
        P("seg", "slab", None, None),
        P("seg", "slab", None, None),
        P(),
        P(),
        P(),
        P("seg", "slab"),
        P("seg", "slab"),
        P("seg", "slab", None),
        P("seg", "slab", None),
        P("seg", "slab", None, None),
        P("seg", "slab", None, None),
        P("seg", "slab", None),
    )
    body = functools.partial(local, mesh.shape["seg"], mesh.shape["slab"])
    return jax.shard_map(
        body, mesh=mesh, in_specs=placed, out_specs=P("seg", "slab", None, None), check_vma=False
    )
```

```python
import functools
import math

import jax
import jax.numpy as jnp
from jax import lax
from jax.experimental import pallas as pl
from jax.experimental.pallas import tpu as pltpu
from jax.sharding import PartitionSpec as P

MESH = pl.DeviceIdType.MESH
HALO = 2
EPSILON2 = 0.05
WALL_GAIN = 3.0
LANES = 128
WIDE = 2 * LANES
TERMS = 16
SPLITS = 3
RAW = 6
PARTS = (2 * WIDE, 4 * WIDE)
CORES = 2
RELAY = 3
RELAY_STEP = 4
F32 = jnp.float32
BF16 = jnp.bfloat16


def up(n, m):
    return -(-n // m) * m


def cuts(n):
    out, start, stop = [], 0, up(n, LANES)
    for width in PARTS + (stop,):
        if start < stop:
            out.append((start, min(width, stop - start)))
            start += out[-1][1]
    return out


def grid(n):
    columns = max(k for k in range(1, n + 1) if n % k == 0 and k * k <= n)
    return n // columns, columns


def split(value, parts):
    out = []
    for _ in range(parts):
        piece = value.astype(BF16).astype(F32)
        out.append(piece)
        value = value - piece
    return out


def spread():
    shape = (3 * TERMS, RAW)
    r, c = (lax.broadcasted_iota(jnp.int32, shape, d) for d in range(2))

    def steps(first, count):
        return sum(jnp.where(r >= first + 3 * (k + 1), 1, 0) for k in range(count))

    at = jnp.where(
        r < 15, 3 + r - 3 * steps(0, 4), jnp.where(
            (r >= 19) & (r < 28), steps(19, 2), jnp.where(
                (r >= 28) & (r < 31), r - 28, jnp.where(
                    (r >= 32) & (r < 35), r - 32, jnp.where((r >= 40) & (r < 43), r - 37, -1)))))
    return jnp.where(c == at, jnp.where((r >= 32) & (r < 35), -2.0, 1.0), 0.0).astype(BF16)


def features(rep, weight):
    lanes = rep.shape[1]
    row = lax.broadcasted_iota(jnp.int32, (8, lanes), 0)
    y2, g = rep[32:40], rep[40:48]
    norm = 0.25 * jnp.sum(y2 * y2, axis=0, keepdims=True)
    dot = -0.5 * weight * jnp.sum(y2 * g, axis=0, keepdims=True)
    m = split(norm + EPSILON2, 3)
    first = jnp.where((row >= 3) & (row < 6), 1.0, y2)
    first = jnp.where(row == 6, m[0], jnp.where(row == 7, m[1], first))
    second = jnp.where(row == 0, m[2], 0.0)
    near = jnp.concatenate([first, second], axis=0).astype(BF16)
    one = rep[0:8] * weight * jnp.where(row < 3, 1.0, rep[16:24])
    two = rep[8:16] * weight * jnp.where(row >= 4, norm, rep[24:32])
    two = two + jnp.where(row >= 4, dot * rep[24:32], 0.0)
    parts = split(jnp.concatenate([one, two], axis=0), SPLITS)
    return near, jnp.concatenate(parts, axis=0).astype(BF16)


def kernel(
    cfg,
    pair_target_far, pair_source_far, junction_cell_far, junction_target_far, wall_near_far,
    positions, density, upsample, quad_far, coarse_far, wall_points, wall_traction,
    out,
    pair_target, pair_source, junction_cell, junction_target, wall_near, quad, coarse,
    own, mine, jsend, jrecv, wall_own, walls, ups, rows, quad_row, coarse_row, xt, xs, held, nears, weights,
    local_sem, halo_send, halo_recv, junction_send, junction_recv, wall_send, wall_recv, column_in, above_in, below_in, *fine,
):
    count, points, fine_points, pairs, near, patch, segs, slabs, per_slab = cfg
    pt, qp = xs.shape[2], quad_row.shape[1]
    rows_t = xt.shape[1]
    seg, slab = lax.axis_index("seg"), lax.axis_index("slab")
    lines, columns = grid(segs)
    levels = slabs // CORES
    line, column = lax.div(seg, columns), lax.rem(seg, columns)
    level, core = lax.div(slab, CORES), lax.rem(slab, CORES)
    partner = slab + 1 - 2 * core
    above, below = level < levels - 1, level > 0

    def turn(base, o, size):
        return lax.rem(base + (o + size), size)

    def across(dy, dx):
        return {"seg": turn(line, dy, lines) * columns + turn(column, dx, columns)}

    barrier = pltpu.get_barrier_semaphore()

    def greet(device):
        pl.semaphore_signal(barrier, inc=1, device_id=device, device_id_type=MESH)

    @pl.when(above)
    def _():
        greet({"slab": slab + CORES})
        greet({"slab": partner + CORES})

    @pl.when(below)
    def _():
        greet({"slab": slab - CORES})
        greet({"slab": partner - CORES})

    for dx in range(1, columns):
        greet(across(0, dx))
    for dy in range(1, lines):
        greet(across(dy, 0))
    greet({"slab": partner})

    copies = [
        pltpu.make_async_copy(positions.at[0], own.at[0], local_sem.at[0]),
        pltpu.make_async_copy(density.at[0], own.at[1], local_sem.at[1]),
        pltpu.make_async_copy(wall_points.at[0], wall_own.at[0], local_sem.at[2]),
        pltpu.make_async_copy(wall_traction.at[0], wall_own.at[1], local_sem.at[3]),
    ]
    big = pltpu.make_async_copy(upsample, ups, local_sem.at[4])
    tables = [
        pltpu.make_async_copy(source, target, local_sem.at[5 + i]) for i, (source, target) in enumerate([
            (pair_target_far, pair_target), (pair_source_far, pair_source), (junction_cell_far, junction_cell),
            (junction_target_far, junction_target), (wall_near_far, wall_near), (quad_far, quad), (coarse_far, coarse)])
    ]
    for copy in copies + tables:
        copy.start()
    big.start()
    for copy in copies + tables:
        copy.wait()

    mine[...] = jnp.zeros_like(mine)

    parts = cuts(fine_points)
    for part in fine:
        @pl.when(slab == 0)
        def _():
            part[0:HALO] = jnp.zeros((HALO,) + part.shape[1:], BF16)

        @pl.when(slab == slabs - 1)
        def _():
            part[HALO + count:] = jnp.zeros((HALO,) + part.shape[1:], BF16)

    coords = [own[0, i].astype(F32) for i in range(3)]
    loads = [own[1, i].astype(F32) for i in range(3)]
    rest = jnp.zeros((8 - RAW, points), F32)
    raws = [jnp.concatenate([line[c:c + 1] for line in coords + loads] + [rest], axis=0) for c in range(count)]
    for c in range(count):
        mine[c, :, 0:points] = raws[c][0:RAW].astype(BF16)
    lhs = jnp.concatenate(raws, axis=0).astype(BF16)
    for b in range(segs):
        jsend[b] = mine[junction_cell[0, 0, b]]
    for p in range(per_slab):
        walls[slab * per_slab + p] = jnp.concatenate(
            [wall_own[0, p].astype(F32), wall_own[1, p].astype(F32)], axis=0).astype(BF16)
    chosen = spread()
    quad_row[...] = jnp.zeros_like(quad_row)
    coarse_row[...] = jnp.zeros_like(coarse_row)
    quad_row[:, 0:fine_points] = quad[...][None]
    coarse_row[:, 0:points] = coarse[...][None]
    rows[...] = jnp.zeros_like(rows)
    xs[...] = jnp.zeros_like(xs)
    norms = split(coords[0] * coords[0] + coords[1] * coords[1] + coords[2] * coords[2], 3)
    rows[6:9] = jnp.ones((3, pt), F32)
    for c in range(count):
        for i in range(3):
            xs[c, i:i + 1, 0:points] = coords[i][c:c + 1]
            rows[i:i + 1, 0:points] = coords[i][c:c + 1]
            rows[3 + i:4 + i, 0:points] = norms[i][c:c + 1]
        xt[c] = rows[...].T[0:rows_t].astype(BF16)

    def refine(p):
        (start, size), part = parts[p], fine[p]
        for at in range(0, size, WIDE):
            stop = min(start + at + WIDE, fine_points)
            value = jnp.dot(lhs, ups[:, start + at:stop], preferred_element_type=F32)
            width = min(WIDE, size - at)
            if stop - start - at < width:
                value = jnp.concatenate([value, jnp.zeros((8 * count, width - value.shape[1]), F32)], axis=1)
            for c in range(count):
                part[HALO + c, :, at:at + width] = value[8 * c:8 * c + RAW].astype(BF16)

    big.wait()
    for p in range(len(fine) - 1):
        refine(p)
    pl.semaphore_wait(barrier, lines - 1 + columns - 1 + 1 + 2 * (jnp.where(above, 1, 0) + jnp.where(below, 1, 0)))

    def halo_up(p):
        return pltpu.make_async_remote_copy(
            fine[p].at[pl.ds(count, HALO)], fine[p].at[pl.ds(0, HALO)], halo_send.at[0, p], halo_recv.at[0, p],
            device_id={"slab": lax.rem(slab + 1, slabs)}, device_id_type=MESH)

    def halo_down(p):
        return pltpu.make_async_remote_copy(
            fine[p].at[pl.ds(HALO, HALO)], fine[p].at[pl.ds(HALO + count, HALO)], halo_send.at[1, p], halo_recv.at[1, p],
            device_id={"slab": lax.rem(slab + slabs - 1, slabs)}, device_id_type=MESH)

    def junction(dy, dx):
        i = dy * columns + dx
        return pltpu.make_async_remote_copy(
            jsend.at[across(dy, dx)["seg"]], jrecv.at[seg], junction_send.at[i], junction_recv.at[i],
            device_id=across(dy, dx), device_id_type=MESH)

    def junction_in(dy, dx):
        i = dy * columns + dx
        return pltpu.make_async_remote_copy(
            jsend.at[seg], jrecv.at[across(-dy, -dx)["seg"]], junction_send.at[i], junction_recv.at[i],
            device_id=across(dy, dx), device_id_type=MESH)

    steps = [(dy, dx) for dy in range(lines) for dx in range(columns) if dy + dx > 0]

    def wall(device):
        slot = pl.ds(slab * per_slab, per_slab)
        return pltpu.make_async_remote_copy(
            walls.at[slot], walls.at[slot], wall_send.at[0], wall_recv.at[0], device_id=device, device_id_type=MESH)

    def walls_all():
        slots = pl.ds(0, (slabs - 1) * per_slab)
        return pltpu.make_async_remote_copy(
            walls.at[slots], walls.at[slots], wall_send.at[0], wall_recv.at[0],
            device_id={"slab": partner}, device_id_type=MESH)

    def wall_to(o):
        @pl.when((level + o >= 0) & (level + o < levels))
        def _():
            wall({"slab": slab + o * CORES}).start()
            wall({"slab": partner + o * CORES}).start()

    def vouch(t):
        @pl.when(below & (level + t < levels))
        def _():
            pl.semaphore_signal(above_in.at[t], inc=1, device_id={"slab": slab - CORES}, device_id_type=MESH)

        @pl.when(above & (level - t >= 0))
        def _():
            pl.semaphore_signal(below_in.at[t], inc=1, device_id={"slab": slab + CORES}, device_id_type=MESH)

    def vouched(t):
        @pl.when(level + 1 + t < levels)
        def _():
            pl.semaphore_wait(above_in.at[t], 1)

        @pl.when(level - 1 - t >= 0)
        def _():
            pl.semaphore_wait(below_in.at[t], 1)

    def send_halo(p):
        pl.when(slab < slabs - 1)(halo_up(p).start)
        pl.when(slab > 0)(halo_down(p).start)

    for dx in range(1, columns):
        pl.semaphore_signal(column_in.at[dx], inc=1, device_id=across(0, dx), device_id_type=MESH)
    vouch(1)
    for p in range(len(fine) - 1):
        send_halo(p)
    for dy, dx in steps:
        if min(dy, dx) == 0:
            junction(dy, dx).start()
    wall({"slab": partner}).start()
    wall_to(1)
    wall_to(-1)
    refine(len(fine) - 1)
    send_halo(len(fine) - 1)
    for dx in range(1, columns):
        pl.semaphore_wait(column_in.at[dx], 1)
        for dy in range(1, lines):
            junction(dy, columns - dx).start()
    for t in range(1, levels - 1):
        vouched(t)
        if t < levels - 2:
            vouch(t + 1)
        wall_to(t + 1)
        wall_to(-1 - t)

    def repeat(raw):
        return jnp.dot(chosen, raw, preferred_element_type=F32)

    def distance(target, near_rows):
        return jnp.dot(xt[target], near_rows, preferred_element_type=F32)

    def weigh(value):
        inverse = lax.rsqrt(value)
        return (inverse * inverse * inverse).astype(BF16)

    def reduce(weights, value):
        sums = lax.dot_general(weights, value, (((1,), (1,)), ((), ())), preferred_element_type=F32)
        return sums[0:TERMS] + sums[TERMS:2 * TERMS] + sums[2 * TERMS:3 * TERMS]

    totals = {}

    def run(units, between):
        before = []
        for k in range(0, len(units) + 2, 2):
            for act in between.get(k // 2, ()):
                act()
            fresh = []
            for u, (item, target, start, size) in enumerate(units[k:k + 2]):
                at = held.at[k // 2 % 2, u, :, 0:size]
                at[...] = weigh(distance(target, nears[:, start:start + size]))
                fresh.append((item, start, size, at))
            for item, start, size, at in before:
                value = reduce(weights[:, start:start + size], at[...])
                totals[item] = totals[item] + value if item in totals else value
            before = fresh

    def prepare(start, rep, weight):
        at = slice(start, start + rep.shape[1])
        nears[:, at], weights[:, at] = features(rep, weight)

    def arrive(p):
        pl.when(slab > 0)(halo_up(p).wait_recv)
        pl.when(slab < slabs - 1)(halo_down(p).wait_recv)

    def prepare_pairs(p):
        start, size = parts[p]
        for k in range(pairs):
            prepare(k * qp + start, repeat(fine[p][pair_source[0, k]]), quad_row[:, start:start + size])

    def prepare_junction(i, dy, dx):
        prepare(pairs * qp + i * pt, repeat(jrecv[across(-dy, -dx)["seg"]]), coarse_row[...])

    def prepare_walls():
        near_by = jnp.concatenate([walls[wall_near[0, n, c]] for c in range(count) for n in range(near)], axis=1)
        prepare(pairs * qp + len(steps) * pt, repeat(near_by), WALL_GAIN)

    steps = sorted(steps, key=lambda step: min(step) > 0)
    direct = [i for i, step in enumerate(steps) if min(step) == 0]
    relayed = [i for i, step in enumerate(steps) if min(step) > 0]

    def arrive_junctions(which):
        for i in which:
            junction_in(*steps[i]).wait_recv()
        for i in which:
            prepare_junction(i, *steps[i])

    units = []
    firsts = []
    for start, size in parts:
        firsts.append(len(units) // 2)
        for at in range(start, start + size, WIDE):
            units += [(("pair", k), pair_target[0, k], k * qp + at, min(WIDE, start + size - at)) for k in range(pairs)]

    def junction_units(which):
        return [
            (("junction",) + steps[i], junction_target[0, 0, across(-steps[i][0], -steps[i][1])["seg"]],
             pairs * qp + i * pt + at, min(WIDE, pt - at)) for at in range(0, pt, WIDE) for i in which]

    ends = [len(units) // 2]
    units += junction_units(direct)
    ends.append(len(units) // 2)
    units += junction_units(relayed)
    ends.append(len(units) // 2)
    base = pairs * qp + len(steps) * pt
    span = near * up(patch, LANES)
    for c in range(count):
        units += [(("wall", c), c, base + c * span + at, min(WIDE, span - at)) for at in range(0, span, WIDE)]

    between = {}

    def when(k, *acts):
        between.setdefault(k, []).extend(acts)

    last = len(parts) - 1
    when(0, *[functools.partial(f, 0) for f in (arrive, prepare_pairs)])
    for p in range(1, len(parts)):
        when(firsts[p - 1], functools.partial(arrive, p))
        when(firsts[p - 1], functools.partial(prepare_pairs, p))
    when(firsts[last], functools.partial(arrive_junctions, direct))
    when(ends[0], functools.partial(arrive_junctions, relayed), walls_all().wait_recv, prepare_walls)
    run(units, between)

    places = [(("pair", k), pair_target[0, k]) for k in range(pairs)]
    places += [(("junction", dy, dx), junction_target[0, 0, across(-dy, -dx)["seg"]]) for dy, dx in steps]
    for c in range(count):
        total = totals["wall", c]
        for item, target in places:
            total = total + jnp.where(target == c, 1.0, 0.0) * totals[item]
        total = total[:, 0:points]
        x = xs[c, :, 0:points]
        x = [x[i:i + 1] for i in range(3)]
        a, b, h = total[0:3], [total[3 + 3 * i:6 + 3 * i] for i in range(3)], total[12:15]
        square = x[0] * x[0] + x[1] * x[1] + x[2] * x[2] + 2.0 * EPSILON2
        value = square * a + h - 2.0 * (x[0] * b[0] + x[1] * b[1] + x[2] * b[2])
        trace = b[0][0:1] + b[1][1:2] + b[2][2:3]
        lift = x[0] * a[0:1] + x[1] * a[1:2] + x[2] * a[2:3] - trace
        for i in range(3):
            along = x[0] * b[i][0:1] + x[1] * b[i][1:2] + x[2] * b[i][2:3]
            out[0, i, c:c + 1] = (value[i:i + 1] + x[i] * lift - along) * (1.0 / (8.0 * math.pi))

    for p in range(len(fine)):
        pl.when(slab < slabs - 1)(halo_up(p).wait_send)
        pl.when(slab > 0)(halo_down(p).wait_send)
    for dy, dx in steps:
        junction(dy, dx).wait_send()
    walls_all().wait_send()


def local(segs, slabs, positions, density, upsample, quad_weights, coarse_weights, pair_target, pair_source,
          junction_cell, junction_target, wall_points, wall_traction, wall_near):
    count, points = positions.shape[1], positions.shape[3]
    turned = (1, 3, count, points)
    fine_points = upsample.shape[1]
    pairs, near = pair_target.shape[1], wall_near.shape[2]
    per_slab, patch = wall_points.shape[1], wall_points.shape[3]
    cfg = (count, points, fine_points, pairs, near, patch, segs, slabs, per_slab)
    pt = up(points, LANES)
    columns, levels = grid(segs)[1], slabs // CORES
    widths = [width for _, width in cuts(fine_points)]
    lanes = pairs * up(fine_points, LANES) + (segs - 1) * pt + count * near * up(patch, LANES)
    vmem = pl.BlockSpec(memory_space=pltpu.VMEM)
    far = pl.BlockSpec(memory_space=pl.ANY)
    dma = pltpu.SemaphoreType.DMA
    result = pl.pallas_call(
        functools.partial(kernel, cfg),
        out_shape=pltpu.VMEM(turned, F32),
        in_specs=[far] * 12,
        out_specs=vmem,
        scratch_shapes=[
            pltpu.SMEM(pair_target.shape, jnp.int32),
            pltpu.SMEM(pair_source.shape, jnp.int32),
            pltpu.SMEM(junction_cell.shape, jnp.int32),
            pltpu.SMEM(junction_target.shape, jnp.int32),
            pltpu.SMEM((1, near, count), jnp.int32),
            pltpu.VMEM(quad_weights.shape, F32),
            pltpu.VMEM(coarse_weights.shape, F32),
            pltpu.VMEM((2,) + turned[1:], BF16),
            pltpu.VMEM((count, RAW, pt), BF16),
            pltpu.VMEM((segs, RAW, pt), BF16),
            pltpu.VMEM((segs, RAW, pt), BF16),
            pltpu.VMEM((2, per_slab, 3, patch), BF16),
            pltpu.VMEM((slabs * per_slab, RAW, patch), BF16),
            pltpu.VMEM(upsample.shape, BF16),
            pltpu.VMEM((TERMS, pt), F32),
            pltpu.VMEM((1, up(fine_points, LANES)), F32),
            pltpu.VMEM((1, pt), F32),
            pltpu.VMEM((count, up(points, 16), TERMS), BF16),
            pltpu.VMEM((count, 3, pt), F32),
            pltpu.VMEM((2, 2, up(points, 16), WIDE), BF16),
            pltpu.VMEM((TERMS, lanes), BF16),
            pltpu.VMEM((SPLITS * TERMS, lanes), BF16),
            dma((12,)), dma((2, len(widths))), dma((2, len(widths))), dma((segs,)), dma((segs,)), dma((1,)), dma((1,)),
            *[pltpu.SemaphoreType.REGULAR((n,)) for n in (columns, levels, levels)],
            *[pltpu.VMEM((count + 2 * HALO, RAW, width), BF16) for width in widths],
        ],
        compiler_params=pltpu.CompilerParams(collective_id=0, has_side_effects=True),
    )(pair_target, pair_source, junction_cell, junction_target, wall_near.transpose(0, 2, 1),
      positions.transpose(0, 2, 1, 3), density.transpose(0, 2, 1, 3), upsample, quad_weights, coarse_weights,
      wall_points, wall_traction)
    return result.transpose(0, 2, 1, 3)


def solution(mesh):
    placed = (
        P("seg", "slab", None, None),
        P("seg", "slab", None, None),
        P(),
        P(),
        P(),
        P("seg", "slab"),
        P("seg", "slab"),
        P("seg", "slab", None),
        P("seg", "slab", None),
        P("seg", "slab", None, None),
        P("seg", "slab", None, None),
        P("seg", "slab", None),
    )
    body = functools.partial(local, mesh.shape["seg"], mesh.shape["slab"])
    return jax.shard_map(
        body, mesh=mesh, in_specs=placed, out_specs=P("seg", "slab", None, None), check_vma=False
    )
```

```python
import functools
import math

import jax
import jax.numpy as jnp
from jax import lax
from jax.experimental import pallas as pl
from jax.experimental.pallas import tpu as pltpu
from jax.sharding import PartitionSpec as P

MESH = pl.DeviceIdType.MESH
HALO = 2
EPSILON2 = 0.05
WALL_GAIN = 3.0
LANES = 128
WIDE = 2 * LANES
TERMS = 16
SPLITS = 3
RAW = 6
PARTS = (2 * WIDE, 4 * WIDE)
CORES = 2
RELAY = 3
RELAY_STEP = 4
F32 = jnp.float32
BF16 = jnp.bfloat16


def up(n, m):
    return -(-n // m) * m


def cuts(n):
    out, start, stop = [], 0, up(n, LANES)
    for width in PARTS + (stop,):
        if start < stop:
            out.append((start, min(width, stop - start)))
            start += out[-1][1]
    return out


def grid(n):
    columns = max(k for k in range(1, n + 1) if n % k == 0 and k * k <= n)
    return n // columns, columns


def split(value, parts):
    out = []
    for _ in range(parts):
        piece = value.astype(BF16).astype(F32)
        out.append(piece)
        value = value - piece
    return out


def spread():
    shape = (3 * TERMS, RAW)
    r, c = (lax.broadcasted_iota(jnp.int32, shape, d) for d in range(2))

    def steps(first, count):
        return sum(jnp.where(r >= first + 3 * (k + 1), 1, 0) for k in range(count))

    at = jnp.where(
        r < 15, 3 + r - 3 * steps(0, 4), jnp.where(
            (r >= 19) & (r < 28), steps(19, 2), jnp.where(
                (r >= 28) & (r < 31), r - 28, jnp.where(
                    (r >= 32) & (r < 35), r - 32, jnp.where((r >= 40) & (r < 43), r - 37, -1)))))
    return jnp.where(c == at, jnp.where((r >= 32) & (r < 35), -2.0, 1.0), 0.0).astype(BF16)


def features(rep, weight):
    lanes = rep.shape[1]
    row = lax.broadcasted_iota(jnp.int32, (8, lanes), 0)
    y2, g = rep[32:40], rep[40:48]
    norm = 0.25 * jnp.sum(y2 * y2, axis=0, keepdims=True)
    dot = -0.5 * weight * jnp.sum(y2 * g, axis=0, keepdims=True)
    m = split(norm + EPSILON2, 3)
    first = jnp.where((row >= 3) & (row < 6), 1.0, y2)
    first = jnp.where(row == 6, m[0], jnp.where(row == 7, m[1], first))
    second = jnp.where(row == 0, m[2], 0.0)
    near = jnp.concatenate([first, second], axis=0).astype(BF16)
    one = rep[0:8] * weight * jnp.where(row < 3, 1.0, rep[16:24])
    two = rep[8:16] * weight * jnp.where(row >= 4, norm, rep[24:32])
    two = two + jnp.where(row >= 4, dot * rep[24:32], 0.0)
    parts = split(jnp.concatenate([one, two], axis=0), SPLITS)
    return near, jnp.concatenate(parts, axis=0).astype(BF16)


def kernel(
    cfg,
    pair_target_far, pair_source_far, junction_cell_far, junction_target_far, wall_near_far,
    positions, density, upsample, quad_far, coarse_far, wall_points, wall_traction,
    out,
    pair_target, pair_source, junction_cell, junction_target, wall_near, quad, coarse,
    own, mine, jsend, jrecv, wall_own, walls, ups, rows, quad_row, coarse_row, xt, xs, held, nears, weights,
    local_sem, big_sem, halo_send, halo_recv, junction_send, junction_recv, wall_send, wall_recv, column_in, above_in, below_in, *fine,
):
    count, points, fine_points, pairs, near, patch, segs, slabs, per_slab = cfg
    pt, qp = xs.shape[2], quad_row.shape[1]
    rows_t = xt.shape[1]
    seg, slab = lax.axis_index("seg"), lax.axis_index("slab")
    lines, columns = grid(segs)
    levels = slabs // CORES
    line, column = lax.div(seg, columns), lax.rem(seg, columns)
    level, core = lax.div(slab, CORES), lax.rem(slab, CORES)
    partner = slab + 1 - 2 * core
    above, below = level < levels - 1, level > 0

    def turn(base, o, size):
        return lax.rem(base + (o + size), size)

    def across(dy, dx):
        return {"seg": turn(line, dy, lines) * columns + turn(column, dx, columns)}

    barrier = pltpu.get_barrier_semaphore()

    def greet(device):
        pl.semaphore_signal(barrier, inc=1, device_id=device, device_id_type=MESH)

    @pl.when(above)
    def _():
        greet({"slab": slab + CORES})
        greet({"slab": partner + CORES})

    @pl.when(below)
    def _():
        greet({"slab": slab - CORES})
        greet({"slab": partner - CORES})

    for dx in range(1, columns):
        greet(across(0, dx))
    for dy in range(1, lines):
        greet(across(dy, 0))
    greet({"slab": partner})

    copies = [
        pltpu.make_async_copy(positions.at[0], own.at[0], local_sem.at[0]),
        pltpu.make_async_copy(density.at[0], own.at[1], local_sem.at[1]),
        pltpu.make_async_copy(wall_points.at[0], wall_own.at[0], local_sem.at[2]),
        pltpu.make_async_copy(wall_traction.at[0], wall_own.at[1], local_sem.at[3]),
    ]
    big = [
        pltpu.make_async_copy(
            upsample.at[:, start:min(start + size, fine_points)], ups.at[:, start:min(start + size, fine_points)], big_sem.at[i])
        for i, (start, size) in enumerate(cuts(fine_points))]
    tables = [
        pltpu.make_async_copy(source, target, local_sem.at[5 + i]) for i, (source, target) in enumerate([
            (pair_target_far, pair_target), (pair_source_far, pair_source), (junction_cell_far, junction_cell),
            (junction_target_far, junction_target), (wall_near_far, wall_near), (quad_far, quad), (coarse_far, coarse)])
    ]
    for copy in copies + tables + big:
        copy.start()
    for copy in copies + tables:
        copy.wait()

    mine[...] = jnp.zeros_like(mine)

    parts = cuts(fine_points)
    for part in fine:
        @pl.when(slab == 0)
        def _():
            part[0:HALO] = jnp.zeros((HALO,) + part.shape[1:], BF16)

        @pl.when(slab == slabs - 1)
        def _():
            part[HALO + count:] = jnp.zeros((HALO,) + part.shape[1:], BF16)

    coords = [own[0, i].astype(F32) for i in range(3)]
    loads = [own[1, i].astype(F32) for i in range(3)]
    rest = jnp.zeros((8 - RAW, points), F32)
    raws = [jnp.concatenate([line[c:c + 1] for line in coords + loads] + [rest], axis=0) for c in range(count)]
    for c in range(count):
        mine[c, :, 0:points] = raws[c][0:RAW].astype(BF16)
    lhs = jnp.concatenate(raws, axis=0).astype(BF16)
    for b in range(segs):
        jsend[b] = mine[junction_cell[0, 0, b]]
    for p in range(per_slab):
        walls[slab * per_slab + p] = jnp.concatenate(
            [wall_own[0, p].astype(F32), wall_own[1, p].astype(F32)], axis=0).astype(BF16)
    def refine(p):
        (start, size), part = parts[p], fine[p]
        big[p].wait()
        for at in range(0, size, WIDE):
            stop = min(start + at + WIDE, fine_points)
            value = jnp.dot(lhs, ups[:, start + at:stop], preferred_element_type=F32)
            width = min(WIDE, size - at)
            if stop - start - at < width:
                value = jnp.concatenate([value, jnp.zeros((8 * count, width - value.shape[1]), F32)], axis=1)
            for c in range(count):
                part[HALO + c, :, at:at + width] = value[8 * c:8 * c + RAW].astype(BF16)

    early = min(0, len(fine))
    for p in range(early):
        refine(p)
    pl.semaphore_wait(barrier, lines - 1 + columns - 1 + 1 + 2 * (jnp.where(above, 1, 0) + jnp.where(below, 1, 0)))

    def halo_up(p):
        return pltpu.make_async_remote_copy(
            fine[p].at[pl.ds(count, HALO)], fine[p].at[pl.ds(0, HALO)], halo_send.at[0, p], halo_recv.at[0, p],
            device_id={"slab": lax.rem(slab + 1, slabs)}, device_id_type=MESH)

    def halo_down(p):
        return pltpu.make_async_remote_copy(
            fine[p].at[pl.ds(HALO, HALO)], fine[p].at[pl.ds(HALO + count, HALO)], halo_send.at[1, p], halo_recv.at[1, p],
            device_id={"slab": lax.rem(slab + slabs - 1, slabs)}, device_id_type=MESH)

    def junction(dy, dx):
        i = dy * columns + dx
        return pltpu.make_async_remote_copy(
            jsend.at[across(dy, dx)["seg"]], jrecv.at[seg], junction_send.at[i], junction_recv.at[i],
            device_id=across(dy, dx), device_id_type=MESH)

    def junction_in(dy, dx):
        i = dy * columns + dx
        return pltpu.make_async_remote_copy(
            jsend.at[seg], jrecv.at[across(-dy, -dx)["seg"]], junction_send.at[i], junction_recv.at[i],
            device_id=across(dy, dx), device_id_type=MESH)

    steps = [(dy, dx) for dy in range(lines) for dx in range(columns) if dy + dx > 0]

    def wall(device):
        slot = pl.ds(slab * per_slab, per_slab)
        return pltpu.make_async_remote_copy(
            walls.at[slot], walls.at[slot], wall_send.at[0], wall_recv.at[0], device_id=device, device_id_type=MESH)

    def walls_all():
        slots = pl.ds(0, (slabs - 1) * per_slab)
        return pltpu.make_async_remote_copy(
            walls.at[slots], walls.at[slots], wall_send.at[0], wall_recv.at[0],
            device_id={"slab": partner}, device_id_type=MESH)

    def wall_to(o):
        @pl.when((level + o >= 0) & (level + o < levels))
        def _():
            wall({"slab": slab + o * CORES}).start()
            wall({"slab": partner + o * CORES}).start()

    def vouch(t):
        @pl.when(below & (level + t < levels))
        def _():
            pl.semaphore_signal(above_in.at[t], inc=1, device_id={"slab": slab - CORES}, device_id_type=MESH)

        @pl.when(above & (level - t >= 0))
        def _():
            pl.semaphore_signal(below_in.at[t], inc=1, device_id={"slab": slab + CORES}, device_id_type=MESH)

    def vouched(t):
        @pl.when(level + 1 + t < levels)
        def _():
            pl.semaphore_wait(above_in.at[t], 1)

        @pl.when(level - 1 - t >= 0)
        def _():
            pl.semaphore_wait(below_in.at[t], 1)

    def send_halo(p):
        pl.when(slab < slabs - 1)(halo_up(p).start)
        pl.when(slab > 0)(halo_down(p).start)

    for dx in range(1, columns):
        pl.semaphore_signal(column_in.at[dx], inc=1, device_id=across(0, dx), device_id_type=MESH)
    vouch(1)
    for p in range(early):
        send_halo(p)
    for dy, dx in steps:
        if min(dy, dx) == 0:
            junction(dy, dx).start()
    wall({"slab": partner}).start()
    wall_to(1)
    wall_to(-1)
    def cross():
        for dx in range(1, columns):
            pl.semaphore_wait(column_in.at[dx], 1)
            for dy in range(1, lines):
                junction(dy, columns - dx).start()

    def reach(stages):
        for t in stages:
            vouched(t)
            if t < levels - 2:
                vouch(t + 1)
            wall_to(t + 1)
            wall_to(-1 - t)

    def halo(chosen_parts):
        for p in chosen_parts:
            refine(p)
            send_halo(p)

    stages, every = range(1, levels - 1), range(len(fine))
    halo(every[0:1])
    halo(every[1:2])
    halo(every[2:])
    chosen = spread()
    quad_row[...] = jnp.zeros_like(quad_row)
    coarse_row[...] = jnp.zeros_like(coarse_row)
    quad_row[:, 0:fine_points] = quad[...][None]
    coarse_row[:, 0:points] = coarse[...][None]
    rows[...] = jnp.zeros_like(rows)
    xs[...] = jnp.zeros_like(xs)
    norms = split(coords[0] * coords[0] + coords[1] * coords[1] + coords[2] * coords[2], 3)
    rows[6:9] = jnp.ones((3, pt), F32)
    for c in range(count):
        for i in range(3):
            xs[c, i:i + 1, 0:points] = coords[i][c:c + 1]
            rows[i:i + 1, 0:points] = coords[i][c:c + 1]
            rows[3 + i:4 + i, 0:points] = norms[i][c:c + 1]
        xt[c] = rows[...].T[0:rows_t].astype(BF16)

    reach(stages[0:1])
    cross()
    def repeat(raw):
        return jnp.dot(chosen, raw, preferred_element_type=F32)

    def distance(target, near_rows):
        return jnp.dot(xt[target], near_rows, preferred_element_type=F32)

    def weigh(value):
        inverse = lax.rsqrt(value)
        return (inverse * inverse * inverse).astype(BF16)

    def reduce(weights, value):
        sums = lax.dot_general(weights, value, (((1,), (1,)), ((), ())), preferred_element_type=F32)
        return sums[0:TERMS] + sums[TERMS:2 * TERMS] + sums[2 * TERMS:3 * TERMS]

    totals = {}

    def run(units, between):
        before = []
        for k in range(0, len(units) + 2, 2):
            for act in between.get(k // 2, ()):
                act()
            fresh = []
            for u, (item, target, start, size) in enumerate(units[k:k + 2]):
                at = held.at[k // 2 % 2, u, :, 0:size]
                at[...] = weigh(distance(target, nears[:, start:start + size]))
                fresh.append((item, start, size, at))
            for item, start, size, at in before:
                value = reduce(weights[:, start:start + size], at[...])
                totals[item] = totals[item] + value if item in totals else value
            before = fresh

    def prepare(start, rep, weight):
        at = slice(start, start + rep.shape[1])
        nears[:, at], weights[:, at] = features(rep, weight)

    def arrive(p):
        pl.when(slab > 0)(halo_up(p).wait_recv)
        pl.when(slab < slabs - 1)(halo_down(p).wait_recv)

    def prepare_pairs(p):
        start, size = parts[p]
        for k in range(pairs):
            prepare(k * qp + start, repeat(fine[p][pair_source[0, k]]), quad_row[:, start:start + size])

    def prepare_junction(i, dy, dx):
        prepare(pairs * qp + i * pt, repeat(jrecv[across(-dy, -dx)["seg"]]), coarse_row[...])

    def prepare_walls():
        near_by = jnp.concatenate([walls[wall_near[0, n, c]] for c in range(count) for n in range(near)], axis=1)
        prepare(pairs * qp + len(steps) * pt, repeat(near_by), WALL_GAIN)

    steps = sorted(steps, key=lambda step: min(step) > 0)
    direct = [i for i, step in enumerate(steps) if min(step) == 0]
    relayed = [i for i, step in enumerate(steps) if min(step) > 0]

    def arrive_junctions(which):
        for i in which:
            junction_in(*steps[i]).wait_recv()
        for i in which:
            prepare_junction(i, *steps[i])

    units = []
    firsts = []
    for start, size in parts:
        firsts.append(len(units) // 2)
        for at in range(start, start + size, WIDE):
            units += [(("pair", k), pair_target[0, k], k * qp + at, min(WIDE, start + size - at)) for k in range(pairs)]

    def junction_units(which):
        return [
            (("junction",) + steps[i], junction_target[0, 0, across(-steps[i][0], -steps[i][1])["seg"]],
             pairs * qp + i * pt + at, min(WIDE, pt - at)) for at in range(0, pt, WIDE) for i in which]

    ends = [len(units) // 2]
    units += junction_units(direct)
    ends.append(len(units) // 2)
    units += junction_units(relayed)
    ends.append(len(units) // 2)
    base = pairs * qp + len(steps) * pt
    span = near * up(patch, LANES)
    for c in range(count):
        units += [(("wall", c), c, base + c * span + at, min(WIDE, span - at)) for at in range(0, span, WIDE)]

    between = {}

    def when(k, *acts):
        between.setdefault(k, []).extend(acts)

    last = len(parts) - 1
    when(0, *[functools.partial(f, 0) for f in (arrive, prepare_pairs)])
    when(0, functools.partial(reach, stages[1:]))
    for p in range(1, len(parts)):
        when(firsts[p - 1], functools.partial(arrive, p))
        when(firsts[p - 1], functools.partial(prepare_pairs, p))
    when(firsts[last], functools.partial(arrive_junctions, direct))
    when(ends[0], functools.partial(arrive_junctions, relayed), walls_all().wait_recv, prepare_walls)
    run(units, between)

    places = [(("pair", k), pair_target[0, k]) for k in range(pairs)]
    places += [(("junction", dy, dx), junction_target[0, 0, across(-dy, -dx)["seg"]]) for dy, dx in steps]
    for c in range(count):
        total = totals["wall", c]
        for item, target in places:
            total = total + jnp.where(target == c, 1.0, 0.0) * totals[item]
        total = total[:, 0:points]
        x = xs[c, :, 0:points]
        x = [x[i:i + 1] for i in range(3)]
        a, b, h = total[0:3], [total[3 + 3 * i:6 + 3 * i] for i in range(3)], total[12:15]
        square = x[0] * x[0] + x[1] * x[1] + x[2] * x[2] + 2.0 * EPSILON2
        value = square * a + h - 2.0 * (x[0] * b[0] + x[1] * b[1] + x[2] * b[2])
        trace = b[0][0:1] + b[1][1:2] + b[2][2:3]
        lift = x[0] * a[0:1] + x[1] * a[1:2] + x[2] * a[2:3] - trace
        for i in range(3):
            along = x[0] * b[i][0:1] + x[1] * b[i][1:2] + x[2] * b[i][2:3]
            out[0, i, c:c + 1] = (value[i:i + 1] + x[i] * lift - along) * (1.0 / (8.0 * math.pi))

    for p in range(len(fine)):
        pl.when(slab < slabs - 1)(halo_up(p).wait_send)
        pl.when(slab > 0)(halo_down(p).wait_send)
    for dy, dx in steps:
        junction(dy, dx).wait_send()
    walls_all().wait_send()


def local(segs, slabs, positions, density, upsample, quad_weights, coarse_weights, pair_target, pair_source,
          junction_cell, junction_target, wall_points, wall_traction, wall_near):
    count, points = positions.shape[1], positions.shape[3]
    turned = (1, 3, count, points)
    fine_points = upsample.shape[1]
    pairs, near = pair_target.shape[1], wall_near.shape[2]
    per_slab, patch = wall_points.shape[1], wall_points.shape[3]
    cfg = (count, points, fine_points, pairs, near, patch, segs, slabs, per_slab)
    pt = up(points, LANES)
    columns, levels = grid(segs)[1], slabs // CORES
    widths = [width for _, width in cuts(fine_points)]
    lanes = pairs * up(fine_points, LANES) + (segs - 1) * pt + count * near * up(patch, LANES)
    vmem = pl.BlockSpec(memory_space=pltpu.VMEM)
    far = pl.BlockSpec(memory_space=pl.ANY)
    dma = pltpu.SemaphoreType.DMA
    result = pl.pallas_call(
        functools.partial(kernel, cfg),
        out_shape=pltpu.VMEM(turned, F32),
        in_specs=[far] * 12,
        out_specs=vmem,
        scratch_shapes=[
            pltpu.SMEM(pair_target.shape, jnp.int32),
            pltpu.SMEM(pair_source.shape, jnp.int32),
            pltpu.SMEM(junction_cell.shape, jnp.int32),
            pltpu.SMEM(junction_target.shape, jnp.int32),
            pltpu.SMEM((1, near, count), jnp.int32),
            pltpu.VMEM(quad_weights.shape, F32),
            pltpu.VMEM(coarse_weights.shape, F32),
            pltpu.VMEM((2,) + turned[1:], BF16),
            pltpu.VMEM((count, RAW, pt), BF16),
            pltpu.VMEM((segs, RAW, pt), BF16),
            pltpu.VMEM((segs, RAW, pt), BF16),
            pltpu.VMEM((2, per_slab, 3, patch), BF16),
            pltpu.VMEM((slabs * per_slab, RAW, patch), BF16),
            pltpu.VMEM(upsample.shape, BF16),
            pltpu.VMEM((TERMS, pt), F32),
            pltpu.VMEM((1, up(fine_points, LANES)), F32),
            pltpu.VMEM((1, pt), F32),
            pltpu.VMEM((count, up(points, 16), TERMS), BF16),
            pltpu.VMEM((count, 3, pt), F32),
            pltpu.VMEM((2, 2, up(points, 16), WIDE), BF16),
            pltpu.VMEM((TERMS, lanes), BF16),
            pltpu.VMEM((SPLITS * TERMS, lanes), BF16),
            dma((12,)), dma((len(widths),)), dma((2, len(widths))), dma((2, len(widths))), dma((segs,)), dma((segs,)), dma((1,)), dma((1,)),
            *[pltpu.SemaphoreType.REGULAR((n,)) for n in (columns, levels, levels)],
            *[pltpu.VMEM((count + 2 * HALO, RAW, width), BF16) for width in widths],
        ],
        compiler_params=pltpu.CompilerParams(collective_id=0, has_side_effects=True),
    )(pair_target, pair_source, junction_cell, junction_target, wall_near.transpose(0, 2, 1),
      positions.transpose(0, 2, 1, 3), density.transpose(0, 2, 1, 3), upsample, quad_weights, coarse_weights,
      wall_points, wall_traction)
    return result.transpose(0, 2, 1, 3)


def solution(mesh):
    placed = (
        P("seg", "slab", None, None),
        P("seg", "slab", None, None),
        P(),
        P(),
        P(),
        P("seg", "slab"),
        P("seg", "slab"),
        P("seg", "slab", None),
        P("seg", "slab", None),
        P("seg", "slab", None, None),
        P("seg", "slab", None, None),
        P("seg", "slab", None),
    )
    body = functools.partial(local, mesh.shape["seg"], mesh.shape["slab"])
    return jax.shard_map(
        body, mesh=mesh, in_specs=placed, out_specs=P("seg", "slab", None, None), check_vma=False
    )
```

```python
import functools
import math

import jax
import jax.numpy as jnp
from jax import lax
from jax.experimental import pallas as pl
from jax.experimental.pallas import tpu as pltpu
from jax.sharding import PartitionSpec as P

MESH = pl.DeviceIdType.MESH
HALO = 2
EPSILON2 = 0.05
WALL_GAIN = 3.0
LANES = 128
WIDE = 2 * LANES
TERMS = 16
SPLITS = 3
RAW = 6
PARTS = (2 * WIDE, 4 * WIDE)
CORES = 2
RELAY = 3
RELAY_STEP = 4
F32 = jnp.float32
BF16 = jnp.bfloat16


def up(n, m):
    return -(-n // m) * m


def cuts(n):
    out, start, stop = [], 0, up(n, LANES)
    for width in PARTS + (stop,):
        if start < stop:
            out.append((start, min(width, stop - start)))
            start += out[-1][1]
    return out


def grid(n):
    columns = max(k for k in range(1, n + 1) if n % k == 0 and k * k <= n)
    return n // columns, columns


def split(value, parts):
    out = []
    for _ in range(parts):
        piece = value.astype(BF16).astype(F32)
        out.append(piece)
        value = value - piece
    return out


def spread():
    shape = (3 * TERMS, RAW)
    r, c = (lax.broadcasted_iota(jnp.int32, shape, d) for d in range(2))

    def steps(first, count):
        return sum(jnp.where(r >= first + 3 * (k + 1), 1, 0) for k in range(count))

    at = jnp.where(
        r < 15, 3 + r - 3 * steps(0, 4), jnp.where(
            (r >= 19) & (r < 28), steps(19, 2), jnp.where(
                (r >= 28) & (r < 31), r - 28, jnp.where(
                    (r >= 32) & (r < 35), r - 32, jnp.where((r >= 40) & (r < 43), r - 37, -1)))))
    return jnp.where(c == at, jnp.where((r >= 32) & (r < 35), -2.0, 1.0), 0.0).astype(BF16)


def features(rep, weight):
    lanes = rep.shape[1]
    row = lax.broadcasted_iota(jnp.int32, (8, lanes), 0)
    y2, g = rep[32:40], rep[40:48]
    norm = 0.25 * jnp.sum(y2 * y2, axis=0, keepdims=True)
    dot = -0.5 * weight * jnp.sum(y2 * g, axis=0, keepdims=True)
    m = split(norm + EPSILON2, 3)
    first = jnp.where((row >= 3) & (row < 6), 1.0, y2)
    first = jnp.where(row == 6, m[0], jnp.where(row == 7, m[1], first))
    second = jnp.where(row == 0, m[2], 0.0)
    near = jnp.concatenate([first, second], axis=0).astype(BF16)
    one = rep[0:8] * weight * jnp.where(row < 3, 1.0, rep[16:24])
    two = rep[8:16] * weight * jnp.where(row >= 4, norm, rep[24:32])
    two = two + jnp.where(row >= 4, dot * rep[24:32], 0.0)
    parts = split(jnp.concatenate([one, two], axis=0), SPLITS)
    return near, jnp.concatenate(parts, axis=0).astype(BF16)


def kernel(
    cfg,
    pair_target_far, pair_source_far, junction_cell_far, junction_target_far, wall_near_far,
    positions, density, upsample, quad_far, coarse_far, wall_points, wall_traction,
    out,
    pair_target, pair_source, junction_cell, junction_target, wall_near, quad, coarse,
    own, mine, jsend, jrecv, wall_own, walls, ups, rows, quad_row, coarse_row, xt, xs, held, nears, weights,
    local_sem, big_sem, halo_send, halo_recv, junction_send, junction_recv, wall_send, wall_recv, column_in, above_in, below_in, *fine,
):
    count, points, fine_points, pairs, near, patch, segs, slabs, per_slab = cfg
    pt, qp = xs.shape[2], quad_row.shape[1]
    rows_t = xt.shape[1]
    seg, slab = lax.axis_index("seg"), lax.axis_index("slab")
    lines, columns = grid(segs)
    levels = slabs // CORES
    line, column = lax.div(seg, columns), lax.rem(seg, columns)
    level, core = lax.div(slab, CORES), lax.rem(slab, CORES)
    partner = slab + 1 - 2 * core
    above, below = level < levels - 1, level > 0

    def turn(base, o, size):
        return lax.rem(base + (o + size), size)

    def across(dy, dx):
        return {"seg": turn(line, dy, lines) * columns + turn(column, dx, columns)}

    barrier = pltpu.get_barrier_semaphore()

    def greet(device):
        pl.semaphore_signal(barrier, inc=1, device_id=device, device_id_type=MESH)

    @pl.when(above)
    def _():
        greet({"slab": slab + CORES})
        greet({"slab": partner + CORES})

    @pl.when(below)
    def _():
        greet({"slab": slab - CORES})
        greet({"slab": partner - CORES})

    for dx in range(1, columns):
        greet(across(0, dx))
    for dy in range(1, lines):
        greet(across(dy, 0))
    greet({"slab": partner})

    copies = [
        pltpu.make_async_copy(positions.at[0], own.at[0], local_sem.at[0]),
        pltpu.make_async_copy(density.at[0], own.at[1], local_sem.at[1]),
        pltpu.make_async_copy(wall_points.at[0], wall_own.at[0], local_sem.at[2]),
        pltpu.make_async_copy(wall_traction.at[0], wall_own.at[1], local_sem.at[3]),
    ]
    big = [
        pltpu.make_async_copy(
            upsample.at[:, start:min(start + size, fine_points)], ups.at[:, start:min(start + size, fine_points)], big_sem.at[i])
        for i, (start, size) in enumerate(cuts(fine_points))]
    tables = [
        pltpu.make_async_copy(source, target, local_sem.at[5 + i]) for i, (source, target) in enumerate([
            (pair_target_far, pair_target), (pair_source_far, pair_source), (junction_cell_far, junction_cell),
            (junction_target_far, junction_target), (wall_near_far, wall_near), (quad_far, quad), (coarse_far, coarse)])
    ]
    for copy in copies + tables + big:
        copy.start()
    for copy in copies + tables:
        copy.wait()

    mine[...] = jnp.zeros_like(mine)

    parts = cuts(fine_points)
    for part in fine:
        @pl.when(slab == 0)
        def _():
            part[0:HALO] = jnp.zeros((HALO,) + part.shape[1:], BF16)

        @pl.when(slab == slabs - 1)
        def _():
            part[HALO + count:] = jnp.zeros((HALO,) + part.shape[1:], BF16)

    coords = [own[0, i].astype(F32) for i in range(3)]
    loads = [own[1, i].astype(F32) for i in range(3)]
    rest = jnp.zeros((8 - RAW, points), F32)
    raws = [jnp.concatenate([line[c:c + 1] for line in coords + loads] + [rest], axis=0) for c in range(count)]
    for c in range(count):
        mine[c, :, 0:points] = raws[c][0:RAW].astype(BF16)
    lhs = jnp.concatenate(raws, axis=0).astype(BF16)
    for b in range(segs):
        jsend[b] = mine[junction_cell[0, 0, b]]
    for p in range(per_slab):
        walls[slab * per_slab + p] = jnp.concatenate(
            [wall_own[0, p].astype(F32), wall_own[1, p].astype(F32)], axis=0).astype(BF16)
    def refine(p):
        (start, size), part = parts[p], fine[p]
        big[p].wait()
        for at in range(0, size, WIDE):
            stop = min(start + at + WIDE, fine_points)
            value = jnp.dot(lhs, ups[:, start + at:stop], preferred_element_type=F32)
            width = min(WIDE, size - at)
            if stop - start - at < width:
                value = jnp.concatenate([value, jnp.zeros((8 * count, width - value.shape[1]), F32)], axis=1)
            for c in range(count):
                part[HALO + c, :, at:at + width] = value[8 * c:8 * c + RAW].astype(BF16)

    early = min(0, len(fine))
    for p in range(early):
        refine(p)
    pl.semaphore_wait(barrier, lines - 1 + columns - 1 + 1 + 2 * (jnp.where(above, 1, 0) + jnp.where(below, 1, 0)))

    def halo_up(p):
        return pltpu.make_async_remote_copy(
            fine[p].at[pl.ds(count, HALO)], fine[p].at[pl.ds(0, HALO)], halo_send.at[0, p], halo_recv.at[0, p],
            device_id={"slab": lax.rem(slab + 1, slabs)}, device_id_type=MESH)

    def halo_down(p):
        return pltpu.make_async_remote_copy(
            fine[p].at[pl.ds(HALO, HALO)], fine[p].at[pl.ds(HALO + count, HALO)], halo_send.at[1, p], halo_recv.at[1, p],
            device_id={"slab": lax.rem(slab + slabs - 1, slabs)}, device_id_type=MESH)

    def junction(dy, dx):
        i = dy * columns + dx
        return pltpu.make_async_remote_copy(
            jsend.at[across(dy, dx)["seg"]], jrecv.at[seg], junction_send.at[i], junction_recv.at[i],
            device_id=across(dy, dx), device_id_type=MESH)

    def junction_in(dy, dx):
        i = dy * columns + dx
        return pltpu.make_async_remote_copy(
            jsend.at[seg], jrecv.at[across(-dy, -dx)["seg"]], junction_send.at[i], junction_recv.at[i],
            device_id=across(dy, dx), device_id_type=MESH)

    steps = [(dy, dx) for dy in range(lines) for dx in range(columns) if dy + dx > 0]

    def wall(device):
        slot = pl.ds(slab * per_slab, per_slab)
        return pltpu.make_async_remote_copy(
            walls.at[slot], walls.at[slot], wall_send.at[0], wall_recv.at[0], device_id=device, device_id_type=MESH)

    def walls_all():
        slots = pl.ds(0, (slabs - 1) * per_slab)
        return pltpu.make_async_remote_copy(
            walls.at[slots], walls.at[slots], wall_send.at[0], wall_recv.at[0],
            device_id={"slab": partner}, device_id_type=MESH)

    def wall_to(o):
        @pl.when((level + o >= 0) & (level + o < levels))
        def _():
            wall({"slab": slab + o * CORES}).start()
            wall({"slab": partner + o * CORES}).start()

    def vouch(t):
        @pl.when(below & (level + t < levels))
        def _():
            pl.semaphore_signal(above_in.at[t], inc=1, device_id={"slab": slab - CORES}, device_id_type=MESH)

        @pl.when(above & (level - t >= 0))
        def _():
            pl.semaphore_signal(below_in.at[t], inc=1, device_id={"slab": slab + CORES}, device_id_type=MESH)

    def vouched(t):
        @pl.when(level + 1 + t < levels)
        def _():
            pl.semaphore_wait(above_in.at[t], 1)

        @pl.when(level - 1 - t >= 0)
        def _():
            pl.semaphore_wait(below_in.at[t], 1)

    def send_halo(p):
        pl.when(slab < slabs - 1)(halo_up(p).start)
        pl.when(slab > 0)(halo_down(p).start)

    for dx in range(1, columns):
        pl.semaphore_signal(column_in.at[dx], inc=1, device_id=across(0, dx), device_id_type=MESH)
    vouch(1)
    for p in range(early):
        send_halo(p)
    for dy, dx in steps:
        if min(dy, dx) == 0:
            junction(dy, dx).start()
    wall({"slab": partner}).start()
    wall_to(1)
    wall_to(-1)
    def cross():
        for dx in range(1, columns):
            pl.semaphore_wait(column_in.at[dx], 1)
            for dy in range(1, lines):
                junction(dy, columns - dx).start()

    def reach(stages):
        for t in stages:
            vouched(t)
            if t < levels - 2:
                vouch(t + 1)
            wall_to(t + 1)
            wall_to(-1 - t)

    def halo(chosen_parts):
        for p in chosen_parts:
            refine(p)
            send_halo(p)

    stages, every = range(1, levels - 1), range(len(fine))
    halo(every[0:1])
    halo(every[1:2])
    halo(every[2:])
    chosen = spread()
    quad_row[...] = jnp.zeros_like(quad_row)
    coarse_row[...] = jnp.zeros_like(coarse_row)
    quad_row[:, 0:fine_points] = quad[...][None]
    coarse_row[:, 0:points] = coarse[...][None]
    rows[...] = jnp.zeros_like(rows)
    xs[...] = jnp.zeros_like(xs)
    norms = split(coords[0] * coords[0] + coords[1] * coords[1] + coords[2] * coords[2], 3)
    rows[6:9] = jnp.ones((3, pt), F32)
    for c in range(count):
        for i in range(3):
            xs[c, i:i + 1, 0:points] = coords[i][c:c + 1]
            rows[i:i + 1, 0:points] = coords[i][c:c + 1]
            rows[3 + i:4 + i, 0:points] = norms[i][c:c + 1]
        xt[c] = rows[...].T[0:rows_t].astype(BF16)

    reach(stages[0:1])
    cross()
    def repeat(raw):
        return jnp.dot(chosen, raw, preferred_element_type=F32)

    def distance(target, near_rows):
        return jnp.dot(xt[target], near_rows, preferred_element_type=F32)

    def weigh(value):
        inverse = lax.rsqrt(value)
        return (inverse * inverse * inverse).astype(BF16)

    def reduce(weights, value):
        sums = lax.dot_general(weights, value, (((1,), (1,)), ((), ())), preferred_element_type=F32)
        return sums[0:TERMS] + sums[TERMS:2 * TERMS] + sums[2 * TERMS:3 * TERMS]

    totals = {}

    def run(units, between):
        before = []
        for k in range(0, len(units) + 2, 2):
            for act in between.get(k // 2, ()):
                act()
            fresh = []
            for u, (item, target, start, size) in enumerate(units[k:k + 2]):
                at = held.at[k // 2 % 2, u, :, 0:size]
                at[...] = weigh(distance(target, nears[:, start:start + size]))
                fresh.append((item, start, size, at))
            for item, start, size, at in before:
                value = reduce(weights[:, start:start + size], at[...])
                totals[item] = totals[item] + value if item in totals else value
            before = fresh

    def prepare(start, rep, weight):
        at = slice(start, start + rep.shape[1])
        nears[:, at], weights[:, at] = features(rep, weight)

    def arrive(p):
        pl.when(slab > 0)(halo_up(p).wait_recv)
        pl.when(slab < slabs - 1)(halo_down(p).wait_recv)

    def prepare_pairs(p):
        start, size = parts[p]
        for k in range(pairs):
            prepare(k * qp + start, repeat(fine[p][pair_source[0, k]]), quad_row[:, start:start + size])

    def prepare_junction(i, dy, dx):
        prepare(pairs * qp + i * pt, repeat(jrecv[across(-dy, -dx)["seg"]]), coarse_row[...])

    def prepare_walls():
        near_by = jnp.concatenate([walls[wall_near[0, n, c]] for c in range(count) for n in range(near)], axis=1)
        prepare(pairs * qp + len(steps) * pt, repeat(near_by), WALL_GAIN)

    steps = sorted(steps, key=lambda step: min(step) > 0)
    direct = [i for i, step in enumerate(steps) if min(step) == 0]
    relayed = [i for i, step in enumerate(steps) if min(step) > 0]

    def arrive_junctions(which):
        for i in which:
            junction_in(*steps[i]).wait_recv()
        for i in which:
            prepare_junction(i, *steps[i])

    units = []
    firsts = []
    for start, size in parts:
        firsts.append(len(units) // 2)
        for at in range(start, start + size, WIDE):
            units += [(("pair", k), pair_target[0, k], k * qp + at, min(WIDE, start + size - at)) for k in range(pairs)]

    def junction_units(which):
        return [
            (("junction",) + steps[i], junction_target[0, 0, across(-steps[i][0], -steps[i][1])["seg"]],
             pairs * qp + i * pt + at, min(WIDE, pt - at)) for at in range(0, pt, WIDE) for i in which]

    ends = [len(units) // 2]
    units += junction_units(direct)
    ends.append(len(units) // 2)
    units += junction_units(relayed)
    ends.append(len(units) // 2)
    base = pairs * qp + len(steps) * pt
    span = near * up(patch, LANES)
    for c in range(count):
        units += [(("wall", c), c, base + c * span + at, min(WIDE, span - at)) for at in range(0, span, WIDE)]

    between = {}

    def when(k, *acts):
        between.setdefault(k, []).extend(acts)

    last = len(parts) - 1
    when(0, *[functools.partial(f, 0) for f in (arrive, prepare_pairs)])
    when(0, functools.partial(reach, stages[1:]))
    for p in range(1, len(parts)):
        when(firsts[p - 1], functools.partial(arrive, p))
        when(firsts[p - 1], functools.partial(prepare_pairs, p))
    when(firsts[last], functools.partial(arrive_junctions, direct))
    when(ends[0], functools.partial(arrive_junctions, relayed))
    when(ends[1], walls_all().wait_recv, prepare_walls)
    run(units, between)

    places = [(("pair", k), pair_target[0, k]) for k in range(pairs)]
    places += [(("junction", dy, dx), junction_target[0, 0, across(-dy, -dx)["seg"]]) for dy, dx in steps]
    for c in range(count):
        total = totals["wall", c]
        for item, target in places:
            total = total + jnp.where(target == c, 1.0, 0.0) * totals[item]
        total = total[:, 0:points]
        x = xs[c, :, 0:points]
        x = [x[i:i + 1] for i in range(3)]
        a, b, h = total[0:3], [total[3 + 3 * i:6 + 3 * i] for i in range(3)], total[12:15]
        square = x[0] * x[0] + x[1] * x[1] + x[2] * x[2] + 2.0 * EPSILON2
        value = square * a + h - 2.0 * (x[0] * b[0] + x[1] * b[1] + x[2] * b[2])
        trace = b[0][0:1] + b[1][1:2] + b[2][2:3]
        lift = x[0] * a[0:1] + x[1] * a[1:2] + x[2] * a[2:3] - trace
        for i in range(3):
            along = x[0] * b[i][0:1] + x[1] * b[i][1:2] + x[2] * b[i][2:3]
            out[0, i, c:c + 1] = (value[i:i + 1] + x[i] * lift - along) * (1.0 / (8.0 * math.pi))

    for p in range(len(fine)):
        pl.when(slab < slabs - 1)(halo_up(p).wait_send)
        pl.when(slab > 0)(halo_down(p).wait_send)
    for dy, dx in steps:
        junction(dy, dx).wait_send()
    walls_all().wait_send()


def local(segs, slabs, positions, density, upsample, quad_weights, coarse_weights, pair_target, pair_source,
          junction_cell, junction_target, wall_points, wall_traction, wall_near):
    count, points = positions.shape[1], positions.shape[3]
    turned = (1, 3, count, points)
    fine_points = upsample.shape[1]
    pairs, near = pair_target.shape[1], wall_near.shape[2]
    per_slab, patch = wall_points.shape[1], wall_points.shape[3]
    cfg = (count, points, fine_points, pairs, near, patch, segs, slabs, per_slab)
    pt = up(points, LANES)
    columns, levels = grid(segs)[1], slabs // CORES
    widths = [width for _, width in cuts(fine_points)]
    lanes = pairs * up(fine_points, LANES) + (segs - 1) * pt + count * near * up(patch, LANES)
    vmem = pl.BlockSpec(memory_space=pltpu.VMEM)
    far = pl.BlockSpec(memory_space=pl.ANY)
    dma = pltpu.SemaphoreType.DMA
    result = pl.pallas_call(
        functools.partial(kernel, cfg),
        out_shape=pltpu.VMEM(turned, F32),
        in_specs=[far] * 12,
        out_specs=vmem,
        scratch_shapes=[
            pltpu.SMEM(pair_target.shape, jnp.int32),
            pltpu.SMEM(pair_source.shape, jnp.int32),
            pltpu.SMEM(junction_cell.shape, jnp.int32),
            pltpu.SMEM(junction_target.shape, jnp.int32),
            pltpu.SMEM((1, near, count), jnp.int32),
            pltpu.VMEM(quad_weights.shape, F32),
            pltpu.VMEM(coarse_weights.shape, F32),
            pltpu.VMEM((2,) + turned[1:], BF16),
            pltpu.VMEM((count, RAW, pt), BF16),
            pltpu.VMEM((segs, RAW, pt), BF16),
            pltpu.VMEM((segs, RAW, pt), BF16),
            pltpu.VMEM((2, per_slab, 3, patch), BF16),
            pltpu.VMEM((slabs * per_slab, RAW, patch), BF16),
            pltpu.VMEM(upsample.shape, BF16),
            pltpu.VMEM((TERMS, pt), F32),
            pltpu.VMEM((1, up(fine_points, LANES)), F32),
            pltpu.VMEM((1, pt), F32),
            pltpu.VMEM((count, up(points, 16), TERMS), BF16),
            pltpu.VMEM((count, 3, pt), F32),
            pltpu.VMEM((2, 2, up(points, 16), WIDE), BF16),
            pltpu.VMEM((TERMS, lanes), BF16),
            pltpu.VMEM((SPLITS * TERMS, lanes), BF16),
            dma((12,)), dma((len(widths),)), dma((2, len(widths))), dma((2, len(widths))), dma((segs,)), dma((segs,)), dma((1,)), dma((1,)),
            *[pltpu.SemaphoreType.REGULAR((n,)) for n in (columns, levels, levels)],
            *[pltpu.VMEM((count + 2 * HALO, RAW, width), BF16) for width in widths],
        ],
        compiler_params=pltpu.CompilerParams(collective_id=0, has_side_effects=True),
    )(pair_target, pair_source, junction_cell, junction_target, wall_near.transpose(0, 2, 1),
      positions.transpose(0, 2, 1, 3), density.transpose(0, 2, 1, 3), upsample, quad_weights, coarse_weights,
      wall_points, wall_traction)
    return result.transpose(0, 2, 1, 3)


def solution(mesh):
    placed = (
        P("seg", "slab", None, None),
        P("seg", "slab", None, None),
        P(),
        P(),
        P(),
        P("seg", "slab"),
        P("seg", "slab"),
        P("seg", "slab", None),
        P("seg", "slab", None),
        P("seg", "slab", None, None),
        P("seg", "slab", None, None),
        P("seg", "slab", None),
    )
    body = functools.partial(local, mesh.shape["seg"], mesh.shape["slab"])
    return jax.shard_map(
        body, mesh=mesh, in_specs=placed, out_specs=P("seg", "slab", None, None), check_vma=False
    )
```
